128 devices in a mesh: sky: 4 (over y), tm: 32 (over z, x, core).
Axes of the slice: x: 4, y: 4, z: 4, core: 2. Of those that a mesh axis runs over, the one named last changes fastest.
Arguments:
- attitude: bfloat16 [3, 8192], P(None, 'tm'), may hold values from -6 to 6
- win_start: int32 [8192], P(('sky', 'tm')), may hold values from 0 to 8128
- design: bfloat16 [8192, 256, 192], P(('sky', 'tm')), may hold values from -0.4375 to 0.4375
- obs_value: float32 [8192, 256], P(('sky', 'tm')), may hold values from -6 to 6
- star_design: float32 [8192, 5, 256], P(('sky', 'tm')), may hold values from -8 to 8
- star_local: int32 [8192, 256], P(('sky', 'tm')), may hold values from 0 to 16383
- block_dest: int32 [8192], P(('sky', 'tm')), may hold values from 0 to 3, as said below
- block_count: int32 [128], P(('sky', 'tm')), may hold values from 32 to 64, as said below
Outputs:
- residual_out: float32 [8192, 256], P(('sky', 'tm'))
- star_update: float32 [5, 65536], P(None, ('sky', 'tm'))
The draws below stay inside these ranges and needn't reach their ends.
Inputs may be any that keep to these rules, and one draw needn't show every extreme that they name: `block_count`: every device has at least 32 live blocks, its first ones; some device has all 64. `block_dest`: no group is named by more than 32 of one device's live blocks, and exactly 32 of them name one group, which is the same group for all devices of one tm index.
All inputs are finite; a program needn't handle non-finite values.
Results may differ from the reference program's by a relative error of at most 0.0003.
Values may be sent and summed in bfloat16 or wider, within the bound.
No kernel may reach another device: no remote copies, remote signals or barrier semaphores. Data moves between devices by JAX's collectives and lax.ppermute only.
A program may use at most 128 MiB of HBM per device.

```python
import jax
import jax.numpy as jnp
from jax import lax

ROWS = 256
WIN = 64
COLS = 192
NBLK_DEV = 64
CAP = 32
STAR_DEV = 512
NBLK = 8192
KNOTS = 8192
STAR_GRP = 16384
N_SKY = 4
N_TM = 32


def route_plan(key):
    device_total = N_SKY * N_TM
    block_counts = jax.random.randint(jax.random.fold_in(key, 11), (device_total,), CAP, NBLK_DEV + 1)
    full_device = jax.random.randint(jax.random.fold_in(key, 12), (), 0, device_total)
    block_counts = jnp.where(jnp.arange(device_total) == full_device, NBLK_DEV, block_counts).astype(jnp.int32)
    busy_group = jax.random.randint(jax.random.fold_in(key, 13), (N_TM,), 0, N_SKY)
    scores = jax.random.randint(jax.random.fold_in(key, 14), (device_total, NBLK_DEV), 0, 1 << 20)
    position = jnp.arange(NBLK_DEV, dtype=jnp.int32)
    live_slot = position[None, :] < block_counts[:, None]
    keyed = jnp.where(live_slot, scores, 1 << 20) * NBLK_DEV + position[None, :]
    sort_order = jnp.argsort(keyed, axis=1)
    slot_rank = jnp.argsort(sort_order, axis=1).astype(jnp.int32)
    device_busy = jnp.tile(busy_group, N_SKY)
    other_group = (slot_rank - CAP) % (N_SKY - 1)
    destination = jnp.where(slot_rank < CAP, device_busy[:, None], (device_busy[:, None] + 1 + other_group) % N_SKY)
    return (block_counts, destination.reshape(-1).astype(jnp.int32))


def draw_block_count(key, part):
    return route_plan(key)[0]


def draw_block_dest(key, part):
    return route_plan(key)[1]


def draw_star_design(key, part):
    subkeys = jax.random.split(key, 2)
    block_total = NBLK_DEV * N_SKY * N_TM
    full_shape = (block_total, 5, ROWS)
    normal_draw = jax.random.normal(subkeys[0], full_shape, jnp.float32)
    epoch_time = jax.random.uniform(subkeys[1], (block_total, 1, ROWS), jnp.float32, -1.0, 1.0)
    stacked = jnp.concatenate([normal_draw[:, 0:1], normal_draw[:, 1:2], 0.6 * normal_draw[:, 0:1] + 0.8 * normal_draw[:, 2:3], epoch_time * normal_draw[:, 0:1] + 0.5 * normal_draw[:, 3:4], epoch_time * normal_draw[:, 1:2] + 0.5 * normal_draw[:, 4:5]], axis=1)
    return jnp.clip(stacked, -8.0, 8.0)


def set_ends(values, stream_key, smallest, top_value):
    shape = values.shape
    place = [jax.random.randint(jax.random.fold_in(stream_key, axis), (), 0, shape[axis]) for axis in range(len(shape))]
    values = values.at[tuple(place)].set(smallest)
    longest = shape.index(max(shape))
    place[longest] = (place[longest] + 1) % shape[longest]
    return values.at[tuple(place)].set(top_value)


def level_of(rng, dims, cuts, least, largest):
    def one(dim, parts):
        heights = jax.random.uniform(jax.random.fold_in(jax.random.fold_in(rng, 6), dim), (parts,), jnp.float32, least / len(cuts), largest / len(cuts))
        return jnp.repeat(jnp.exp(heights), dims[dim] // parts).reshape((-1,) + (1,) * (len(dims) - dim - 1))

    loudness = one(*cuts[0])
    for cut in cuts[1:]:
        loudness = loudness * one(*cut)
    return loudness


def bell_draw(stream_key, dims, spread, reach, cuts=(), kind=jnp.bfloat16):
    drawn = jax.random.normal(stream_key, dims, jnp.float32) * spread
    if len(cuts) > 0:
        drawn = level_of(stream_key, dims, cuts, -0.22, 0.18) * drawn
    return jnp.clip(drawn, min=-reach, max=reach).astype(kind)


def setup_inputs(seed: int = 0) -> dict:
    keys = jax.random.split(jax.random.key(seed), 9)
    return {
        "attitude": bell_draw(keys[0], (3, KNOTS), 1.0, 6.0, ((1, 32),)),
        "win_start": set_ends(jax.random.randint(keys[1], (NBLK,), 0, KNOTS - WIN + 1), jax.random.fold_in(keys[1], 1), 0, KNOTS - WIN).astype(jnp.int32),
        "design": bell_draw(keys[2], (NBLK, ROWS, COLS), COLS ** -0.5, 0.4375, ((0, 128),)),
        "obs_value": bell_draw(keys[3], (NBLK, ROWS), 1.0, 6.0, ((0, 128),), jnp.float32),
        "star_design": draw_star_design(jax.random.fold_in(keys[8], 71), 0),
        "star_local": set_ends(jax.random.randint(keys[5], (NBLK, ROWS), 0, STAR_GRP), jax.random.fold_in(keys[5], 1), 0, STAR_GRP - 1).astype(jnp.int32),
        "block_dest": draw_block_dest(jax.random.fold_in(keys[8], 71), 0),
        "block_count": draw_block_count(jax.random.fold_in(keys[8], 71), 0),
    }


ridge_term = 1.0

def pair_terms(partials, values):
    term_list = []
    for i in range(5):
        for j in range(i, 5):
            term_list.append(partials[:, i] * partials[:, j])
    for i in range(5):
        term_list.append(partials[:, i] * values)
    return jnp.stack(term_list).reshape(20, -1)

def solve_five(packed):
    entries = {}
    packed_row = 0
    for i in range(5):
        for j in range(i, 5):
            if i == j:
                entries[i, j] = packed[packed_row] + ridge_term
            else:
                entries[i, j] = packed[packed_row]
            packed_row += 1
    factor = {}
    for j in range(5):
        pivot_value = entries[j, j]
        for k in range(j):
            pivot_value = pivot_value - factor[j, k] * factor[j, k]
        factor[j, j] = jnp.sqrt(pivot_value)
        for i in range(j + 1, 5):
            running_value = entries[j, i]
            for k in range(j):
                running_value = running_value - factor[i, k] * factor[j, k]
            factor[i, j] = running_value / factor[j, j]
    forward = []
    for i in range(5):
        running_value = packed[15 + i]
        for k in range(i):
            running_value = running_value - factor[i, k] * forward[k]
        forward.append(running_value / factor[i, i])
    answer = [None] * 5
    for i in reversed(range(5)):
        running_value = forward[i]
        for k in range(i + 1, 5):
            running_value = running_value - factor[k, i] * answer[k]
        answer[i] = running_value / factor[i, i]
    return jnp.stack(answer)

def star_fit(partials, picked):
    summed = partials[:, 0] * picked[0]
    for c in range(1, 5):
        summed = summed + partials[:, c] * picked[c]
    return summed

def reference(attitude, win_start, design, obs_value, star_design, star_local, block_dest, block_count):
    block_total = design.shape[0]
    groups_count = block_total // NBLK_DEV
    offsets = win_start[:, None] + jnp.arange(WIN, dtype=jnp.int32)[None, :]
    windows = attitude[:, offsets]
    flat_window = jnp.transpose(windows, (1, 0, 2)).reshape(block_total, 3 * WIN)

    def fit_group(pair_input):
        group_design, group_window = pair_input
        return jnp.einsum('brc,bc->br', group_design.astype(jnp.float32), group_window.astype(jnp.float32), precision=lax.Precision.HIGHEST)
    fitted = lax.map(fit_group, (design.reshape(groups_count, NBLK_DEV, ROWS, 3 * WIN), flat_window.reshape(groups_count, NBLK_DEV, 3 * WIN)))
    fitted = fitted.reshape(block_total, ROWS)
    residual = obs_value - fitted
    block_ids = jnp.arange(block_total, dtype=jnp.int32)
    live = block_ids % NBLK_DEV < block_count[block_ids // NBLK_DEV]
    live_weight = live.astype(jnp.float32)
    star_group = STAR_DEV * N_TM
    star_ids = block_dest[:, None] * star_group + star_local
    masked_partials = star_design * live_weight[:, None, None]
    masked_residual = residual * live_weight[:, None]

    def accumulate(running, group_input):
        partials, values, ids = group_input
        return (running.at[:, ids.reshape(-1)].add(pair_terms(partials, values)), None)
    normals, unused = lax.scan(accumulate, jnp.zeros((20, star_group * N_SKY), jnp.float32), (masked_partials.reshape(groups_count, NBLK_DEV, 5, ROWS), masked_residual.reshape(groups_count, NBLK_DEV, ROWS), star_ids.reshape(groups_count, NBLK_DEV, ROWS)))
    star_update = solve_five(normals)
    picked = star_update[:, star_ids]
    updated = residual - star_fit(star_design, picked)
    residual_out = jnp.where(live[:, None], updated, jnp.zeros_like(updated))
    return (residual_out, star_update)
```

```python
import jax
import jax.numpy as jnp
from jax import lax
from jax.experimental import pallas as pl
from jax.experimental.pallas import tpu as pltpu
from jax.sharding import PartitionSpec as P

ROWS = 256
WIN = 64
CAP = 32
NBLK = 64
SLOTS = 128
STAR_DEV = 512
HW = 16
NHI = 64
F32 = jnp.float32
BF16 = jnp.bfloat16
I32 = jnp.int32
VM = pl.BlockSpec(memory_space=pltpu.VMEM)
SM = pl.BlockSpec(memory_space=pltpu.SMEM)


def shape(dims, dtype=F32):
    return jax.ShapeDtypeStruct(dims, dtype)


def pack_kernel(dest, count, partials, stars, out, slots, used):
    out[...] = jnp.zeros_like(out)
    out[:, 160:192, :] = jnp.full((4, 32, ROWS), -1.0, F32)
    for g in range(4):
        used[g] = 0

    def place(b, carry):
        g = dest[b]
        k = used[g]
        used[g] = k + 1
        slots[b] = g * CAP + k
        for q in range(5):
            out[g, pl.ds(q * CAP + k, 1), :] = partials[b, q:q + 1, :]
        out[g, pl.ds(5 * CAP + k, 1), :] = stars[pl.ds(b, 1), :].astype(F32)
        return carry

    lax.fori_loop(0, count[0], place, 0)

    def skip(b, carry):
        slots[b] = -1
        return carry

    lax.fori_loop(count[0], NBLK, skip, 0)


def pack(dest, count, partials, stars):
    return pl.pallas_call(
        pack_kernel,
        name="pack",
        out_shape=(shape((4, 192, ROWS)), shape((NBLK,), I32)),
        in_specs=[SM, SM, VM, VM],
        out_specs=(VM, SM),
        scratch_shapes=[pltpu.SMEM((4,), I32)],
    )(dest, count, partials, stars)


def spread_kernel(slots, count, rows, out):
    out[...] = jnp.zeros_like(out)

    def place(b, carry):
        out[pl.ds(slots[b], 1), :] = rows[pl.ds(b, 1), :]
        return carry

    lax.fori_loop(0, count[0], place, 0)


def spread(slots, count, rows):
    return pl.pallas_call(
        spread_kernel, name="spread", out_shape=shape((SLOTS, ROWS)), in_specs=[SM, SM, VM], out_specs=VM
    )(slots, count, rows)


def collect_kernel(slots, count, rows, out):
    out[...] = jnp.zeros_like(out)

    def place(b, carry):
        out[pl.ds(b, 1), :] = rows[pl.ds(slots[b], 1), :]
        return carry

    lax.fori_loop(0, count[0], place, 0)


def collect(slots, count, rows):
    return pl.pallas_call(
        collect_kernel, name="collect", out_shape=shape((NBLK, ROWS)), in_specs=[SM, SM, VM], out_specs=VM
    )(slots, count, rows)


def window_kernel(start_s, start_v, knots, out, near, far):
    def place(b, carry):
        tile = start_s[b] // 128
        after = jnp.minimum(tile + 1, 63)
        for axis in range(3):
            near[axis, pl.ds(b, 1), :] = knots[tile // 2, pl.ds(3 * (tile % 2) + axis, 1), :]
            far[axis, pl.ds(b, 1), :] = knots[after // 2, pl.ds(3 * (after % 2) + axis, 1), :]
        return carry

    lax.fori_loop(0, NBLK, place, 0)
    lane = lax.broadcasted_iota(I32, (NBLK, 128), 1)
    at = lane + (start_v[...] & 127)
    wrapped = at & 127
    got = []
    for axis in range(3):
        a = jnp.take_along_axis(near[axis], wrapped, axis=1, mode="promise_in_bounds")
        b = jnp.take_along_axis(far[axis], wrapped, axis=1, mode="promise_in_bounds")
        got.append(jnp.where(at < 128, a, b))
    out[:, :128] = jnp.where(lane < WIN, got[0], pltpu.roll(got[1], WIN, 1)).astype(BF16)
    out[:, 128:] = got[2][:, :WIN].astype(BF16)


def windows_of(win_start, knots):
    return pl.pallas_call(
        window_kernel,
        name="windows",
        out_shape=shape((NBLK, 3 * WIN), BF16),
        in_specs=[SM, VM, VM],
        out_specs=VM,
        scratch_shapes=[pltpu.VMEM((3, NBLK, 128), F32), pltpu.VMEM((3, NBLK, 128), F32)],
    )(win_start, win_start.reshape(NBLK, 1), knots)


def sort_rows(cols):
    sub = lax.broadcasted_iota(I32, (8, 128), 0)
    k = 2
    while k <= ROWS:
        j = k // 2
        while j >= 1:
            if j >= 8:
                step = j // 8
                for v in range(32):
                    w = v ^ step
                    if v < w:
                        low = jnp.minimum(cols[v], cols[w])
                        high = jnp.maximum(cols[v], cols[w])
                        up = ((v * 8) & k) == 0
                        cols[v], cols[w] = (low, high) if up else (high, low)
            else:
                first = (sub & j) == 0
                for v in range(32):
                    x = cols[v]
                    if j == 4:
                        other = pltpu.roll(x, 4, 0)
                    else:
                        other = jnp.where(first, pltpu.roll(x, 8 - j, 0), pltpu.roll(x, j, 0))
                    low = jnp.minimum(x, other)
                    high = jnp.maximum(x, other)
                    if k >= 8:
                        take_low = first if ((v * 8) & k) == 0 else jnp.logical_not(first)
                    else:
                        take_low = first == ((sub & k) == 0)
                    cols[v] = jnp.where(take_low, low, high)
            j //= 2
        k *= 2
    return cols


def pick_lanes(x, idx):
    halves = []
    for h in range(2):
        at = idx[:, h * 128:(h + 1) * 128]
        near = at & 127
        a = jnp.take_along_axis(x[:, :128], near, axis=1, mode="promise_in_bounds")
        b = jnp.take_along_axis(x[:, 128:], near, axis=1, mode="promise_in_bounds")
        halves.append(jnp.where(at < 128, a, b))
    return jnp.concatenate(halves, axis=1)


def sort_kernel(inc, sk, skt, idx, inv, ps, bounds):
    ids = jnp.concatenate([inc[s, 160:192, :] for s in range(4)], axis=0)
    key = ids * 256.0 + lax.broadcasted_iota(I32, (SLOTS, ROWS), 1).astype(F32)
    kt = key.T
    skey = jnp.concatenate(sort_rows([kt[8 * v:8 * v + 8] for v in range(32)]), axis=0).astype(I32)
    star = skey >> 8
    sk[...] = star
    place = skey & 255
    hi = star >> 8
    for c in range(32):
        h = hi[8 * c:8 * c + 8]
        s = star[8 * c:8 * c + 8]
        bounds[c] = jnp.min(jnp.where(s >= 0, h, 999))
        bounds[32 + c] = jnp.max(jnp.where(s >= 0, h, -1))
    back = (place * 256 + lax.broadcasted_iota(I32, (ROWS, SLOTS), 0)).astype(F32)
    inv_rows = sort_rows([back[8 * v:8 * v + 8] for v in range(32)])
    inv[...] = (jnp.concatenate(inv_rows, axis=0).astype(I32) & 255).T
    start = star.T
    for h in range(2):
        skt[h] = start[:, h * 128:(h + 1) * 128]
    place_t = place.T
    idx[...] = place_t
    for q in range(5):
        p = jnp.concatenate([inc[s, q * CAP:(q + 1) * CAP, :] for s in range(4)], axis=0)
        ps[q * ROWS:(q + 1) * ROWS] = pick_lanes(p, place_t).T
    ps[5 * ROWS:] = jnp.zeros((3 * ROWS, SLOTS), F32)


def sort_slots(inc):
    return pl.pallas_call(
        sort_kernel,
        name="sort",
        out_shape=(
            shape((ROWS, SLOTS), I32),
            shape((2, 128, 128), I32),
            shape((SLOTS, ROWS), I32),
            shape((SLOTS, ROWS), I32),
            shape((8 * ROWS, SLOTS)),
            shape((64,), I32),
        ),
        in_specs=[VM],
        out_specs=(VM,) * 5 + (SM,),
    )(inc)


def scatter_kernel(bounds, core, sk, skt, idx, ps, res, out, acc, rs, tall, tb, oh, lhs):
    rs[...] = pick_lanes(res[...], idx[...]).T
    acc[...] = jnp.zeros_like(acc)
    rowh = (lax.broadcasted_iota(I32, (80, 128), 0) >= 40).astype(F32).astype(BF16)
    lane = lax.broadcasted_iota(I32, (128, 256), 1).astype(F32).astype(BF16)
    zero = jnp.zeros((), BF16)
    one = jnp.ones((), BF16)

    def chunk(c, carry):
        at = pl.multiple_of(c * 8, 8)
        p = [ps[pl.ds(pl.multiple_of(q * ROWS + c * 8, 8), 8), :] for q in range(5)]
        r = rs[pl.ds(at, 8), :]
        terms = [p[i] * p[j] for i in range(5) for j in range(i, 5)] + [p[i] * r for i in range(5)]
        for t, v in enumerate(terms):
            big = v.astype(BF16).astype(F32)
            tall[pl.ds(t * 8, 8), :] = big
            tall[pl.ds((20 + t) * 8, 8), :] = v - big
        lo = pltpu.roll(skt[c // 16] & 255, 128 - (c % 16) * 8, 1).astype(F32).astype(BF16)
        for s in range(8):
            got = tall[pl.ds(s, 40, stride=8), :].astype(BF16)
            tb[:40, s * 128:(s + 1) * 128] = got
            tb[40:, s * 128:(s + 1) * 128] = got
            col = jnp.broadcast_to(lo[:, s:s + 1], (128, 256))
            oh[s * 128:(s + 1) * 128, :] = jnp.where(col == lane, one, zero)
        h_low = bounds[c]
        hi = sk[pl.ds(at, 8), :] >> 8

        def window(w, carry):
            h0 = h_low + w * HW
            rel = (hi - h0).astype(F32)
            for s in range(8):
                diff = jnp.broadcast_to(rel[s:s + 1, :], (80, 128)).astype(BF16) - rowh
                t = tb[:, s * 128:(s + 1) * 128]
                for j in range(HW // 2):
                    lhs[j * 80:(j + 1) * 80, s * 128:(s + 1) * 128] = jnp.where(diff == 2.0 * j, t, zero)
            prod = jnp.dot(lhs[...], oh[...], preferred_element_type=F32)
            acc[pl.ds(h0, HW)] += prod.reshape(HW, 40, 256)
            return carry

        lax.fori_loop(0, (bounds[32 + c] - h_low) // HW + 1, window, 0)
        return carry

    lax.fori_loop(0, 32, chunk, 0)
    me = core[0]
    for g in range(16):
        for side in range(2):
            t = 2 * g + (me if side == 0 else 1 - me)
            for a in range(2):
                block = acc[2 * t + a]
                out[side, g, a * 20:(a + 1) * 20, :] = block[:20] + block[20:]


def scatter(bounds, core, sk, skt, idx, ps, res):
    return pl.pallas_call(
        scatter_kernel,
        name="scatter",
        out_shape=shape((2, 16, 40, 256)),
        in_specs=[SM, SM] + [VM] * 5,
        out_specs=VM,
        scratch_shapes=[
            pltpu.VMEM((NHI + HW, 40, 256), F32),
            pltpu.VMEM((ROWS, SLOTS), F32),
            pltpu.VMEM((320, 128), F32),
            pltpu.VMEM((80, 1024), BF16),
            pltpu.VMEM((1024, 256), BF16),
            pltpu.VMEM((40 * HW, 1024), BF16),
        ],
    )(bounds, core, sk, skt, idx, ps, res)


def solve_kernel(parts, update, packed, total):
    total[...] = jnp.sum(parts[...], axis=0)

    def row(r):
        return jnp.concatenate([total[r:r + 1, :], total[20 + r:21 + r, :]], axis=0)

    entries = {}
    r = 0
    for i in range(5):
        for j in range(i, 5):
            entries[i, j] = row(r) + 1.0 if i == j else row(r)
            r += 1
    factor = {}
    for j in range(5):
        pivot = entries[j, j]
        for k in range(j):
            pivot = pivot - factor[j, k] * factor[j, k]
        factor[j, j] = jnp.sqrt(pivot)
        for i in range(j + 1, 5):
            running = entries[j, i]
            for k in range(j):
                running = running - factor[i, k] * factor[j, k]
            factor[i, j] = running / factor[j, j]
    forward = []
    for i in range(5):
        running = row(15 + i)
        for k in range(i):
            running = running - factor[i, k] * forward[k]
        forward.append(running / factor[i, i])
    answer = [None] * 5
    for i in reversed(range(5)):
        running = forward[i]
        for k in range(i + 1, 5):
            running = running - factor[k, i] * answer[k]
        answer[i] = running / factor[i, i]
    packed[...] = jnp.zeros_like(packed)
    for i in range(5):
        for a in range(2):
            update[i:i + 1, a * 256:(a + 1) * 256] = answer[i][a:a + 1]
            packed[8 * a + i:8 * a + i + 1, :] = answer[i][a:a + 1]


def solve(parts):
    return pl.pallas_call(
        solve_kernel,
        name="solve",
        out_shape=(shape((5, STAR_DEV)), shape((16, 256))),
        in_specs=[VM],
        out_specs=(VM, VM),
        scratch_shapes=[pltpu.VMEM((40, 256), F32)],
    )(parts)


def fit_kernel(bounds, sk, inv, ps, res, table, out, xb, oh, got, fit):
    big = table[...].astype(BF16).astype(F32)
    xb[:NHI, :8, :] = big.astype(BF16)
    xb[:NHI, 8:, :] = (table[...] - big).astype(BF16)
    xb[NHI:] = jnp.zeros((HW, 16, 256), BF16)
    lo_row = lax.broadcasted_iota(I32, (256, 128), 0).astype(F32).astype(BF16)
    zero = jnp.zeros((), BF16)
    one = jnp.ones((), BF16)

    def chunk(c, carry):
        at = pl.multiple_of(c * 8, 8)
        star = sk[pl.ds(at, 8), :]
        lo = (star & 255).astype(F32)
        hi = star >> 8
        for s in range(8):
            row = jnp.broadcast_to(lo[s:s + 1, :], (256, 128)).astype(BF16)
            oh[:, s * 128:(s + 1) * 128] = jnp.where(row == lo_row, one, zero)
        h_low = bounds[c]

        def window(w, sums):
            h0 = h_low + w * HW
            got[...] = jnp.dot(
                xb[pl.ds(h0, HW)].reshape(HW * 16, 256), oh[...], preferred_element_type=F32
            )
            new = []
            for s in range(8):
                rel = jnp.broadcast_to(hi[s:s + 1, :] - h0, (8, 128))
                total = sums[s]
                for h in range(HW):
                    y = (
                        got[h * 16:h * 16 + 8, s * 128:(s + 1) * 128]
                        + got[h * 16 + 8:h * 16 + 16, s * 128:(s + 1) * 128]
                    )
                    total = jnp.where(rel == h, y, total)
                new.append(total)
            return tuple(new)

        sums = lax.fori_loop(
            0, (bounds[32 + c] - h_low) // HW + 1, window, tuple(jnp.zeros((8, 128), F32) for s in range(8))
        )
        for s in range(8):
            p = ps[pl.ds(c * 8 + s, 8, stride=ROWS), :]
            fit[pl.ds(c * 8 + s, 1), :] = jnp.sum(p * sums[s], axis=0, keepdims=True)
        return carry

    lax.fori_loop(0, 32, chunk, 0)
    out[...] = res[...] - pick_lanes(fit[...].T, inv[...])


def apply_fit(bounds, sk, inv, ps, res, table):
    return pl.pallas_call(
        fit_kernel,
        name="fit",
        out_shape=shape((SLOTS, ROWS)),
        in_specs=[SM] + [VM] * 5,
        out_specs=VM,
        scratch_shapes=[
            pltpu.VMEM((NHI + HW, 16, 256), BF16),
            pltpu.VMEM((256, 1024), BF16),
            pltpu.VMEM((HW * 16, 1024), F32),
            pltpu.VMEM((ROWS, SLOTS), F32),
        ],
    )(bounds, sk, inv, ps, res, table)


def local(attitude, win_start, design, obs_value, star_design, star_local, block_dest, block_count):
    tm = lax.axis_size("tm")
    core = (lax.axis_index("tm") % 2).astype(I32)
    swap = [(i, i ^ 1) for i in range(tm)]
    chips = [list(range(0, tm, 2)), list(range(1, tm, 2))]

    outgoing, slots = pack(block_dest, block_count, star_design, star_local)
    incoming = lax.all_to_all(outgoing, "sky", 0, 0, tiled=True)

    piece = attitude.astype(F32).reshape(3, 2, 128).transpose(1, 0, 2).reshape(6, 128)
    piece = jnp.pad(piece, ((0, 2), (0, 0)))
    knots = lax.all_to_all(jnp.broadcast_to(piece[None], (tm, 8, 128)), "tm", 0, 0, tiled=True)
    windows = windows_of(win_start, knots)
    fitted = jnp.einsum("brc,bc->br", design, windows, preferred_element_type=F32)
    residual = obs_value - fitted
    out_res = spread(slots, block_count, residual)
    in_res = lax.all_to_all(out_res.reshape(4, CAP, ROWS), "sky", 0, 0, tiled=True).reshape(SLOTS, ROWS)

    sk, skt, idx, inv, ps, bounds = sort_slots(incoming)
    partial = scatter(bounds, core[None], sk, skt, idx, ps, in_res)
    pair_sum = partial[0] + lax.ppermute(partial[1], "tm", swap)
    parts = lax.all_to_all(pair_sum, "tm", 0, 0, tiled=True, axis_index_groups=chips)
    own_update, packed = solve(parts)
    other = lax.ppermute(packed, "tm", swap)
    both = jnp.where(core == 0, jnp.stack([packed, other]), jnp.stack([other, packed]))
    table = lax.all_to_all(
        jnp.broadcast_to(both[None], (16, 2, 16, 256)), "tm", 0, 0, tiled=True, axis_index_groups=chips
    ).reshape(NHI, 8, 256)
    updated = apply_fit(bounds, sk, inv, ps, in_res, table)
    returned = lax.all_to_all(updated.reshape(4, CAP, ROWS), "sky", 0, 0, tiled=True).reshape(SLOTS, ROWS)
    result = collect(slots, block_count, returned)
    return (result, own_update)


def solution(mesh):
    placed = (
        P(None, "tm"),
        P(("sky", "tm")),
        P(("sky", "tm"), None, None),
        P(("sky", "tm"), None),
        P(("sky", "tm"), None, None),
        P(("sky", "tm"), None),
        P(("sky", "tm")),
        P(("sky", "tm")),
    )
    return jax.shard_map(
        local,
        mesh=mesh,
        in_specs=placed,
        out_specs=(P(("sky", "tm"), None), P(None, ("sky", "tm"))),
        check_vma=False,
    )
```

```python
import jax
import jax.numpy as jnp
from jax import lax
from jax.experimental import pallas as pl
from jax.experimental.pallas import tpu as pltpu
from jax.sharding import PartitionSpec as P

ROWS = 256
WIN = 64
CAP = 32
NBLK = 64
SLOTS = 128
STAR_DEV = 512
HW = 16
NHI = 64
F32 = jnp.float32
BF16 = jnp.bfloat16
I32 = jnp.int32
VM = pl.BlockSpec(memory_space=pltpu.VMEM)
SM = pl.BlockSpec(memory_space=pltpu.SMEM)


def shape(dims, dtype=F32):
    return jax.ShapeDtypeStruct(dims, dtype)


def pack_kernel(dest, count, partials, stars, out, slots, used):
    out[...] = jnp.zeros_like(out)
    out[:, 160:192, :] = jnp.full((4, 32, ROWS), -1.0, F32)
    for g in range(4):
        used[g] = 0

    def place(b, carry):
        g = dest[b]
        k = used[g]
        used[g] = k + 1
        slots[b] = g * CAP + k
        for q in range(5):
            out[g, pl.ds(q * CAP + k, 1), :] = partials[q, pl.ds(b, 1), :]
        out[g, pl.ds(5 * CAP + k, 1), :] = stars[pl.ds(b, 1), :].astype(F32)
        return carry

    lax.fori_loop(0, count[0], place, 0)

    def skip(b, carry):
        slots[b] = -1
        return carry

    lax.fori_loop(count[0], NBLK, skip, 0)


def pack(dest, count, partials, stars):
    return pl.pallas_call(
        pack_kernel,
        name="pack",
        out_shape=(shape((4, 192, ROWS)), shape((NBLK,), I32)),
        in_specs=[SM, SM, VM, VM],
        out_specs=(VM, SM),
        scratch_shapes=[pltpu.SMEM((4,), I32)],
    )(dest, count, partials, stars)


def spread_kernel(slots, count, rows, out):
    out[...] = jnp.zeros_like(out)

    def place(b, carry):
        out[pl.ds(slots[b], 1), :] = rows[pl.ds(b, 1), :]
        return carry

    lax.fori_loop(0, count[0], place, 0)


def spread(slots, count, rows):
    return pl.pallas_call(
        spread_kernel, name="spread", out_shape=shape((SLOTS, ROWS)), in_specs=[SM, SM, VM], out_specs=VM
    )(slots, count, rows)


def collect_kernel(slots, count, rows, out):
    out[...] = jnp.zeros_like(out)

    def place(b, carry):
        out[pl.ds(b, 1), :] = rows[pl.ds(slots[b], 1), :]
        return carry

    lax.fori_loop(0, count[0], place, 0)


def collect(slots, count, rows):
    return pl.pallas_call(
        collect_kernel, name="collect", out_shape=shape((NBLK, ROWS)), in_specs=[SM, SM, VM], out_specs=VM
    )(slots, count, rows)


def window_kernel(start, knots, out, near, far, shift):
    def place(b, carry):
        tile = start[b] // 128
        shift[pl.ds(b, 1), :] = jnp.full((1, 128), start[b] % 128, I32)
        after = jnp.minimum(tile + 1, 63)
        for axis in range(3):
            near[axis, pl.ds(b, 1), :] = knots[tile // 2, pl.ds(3 * (tile % 2) + axis, 1), :]
            far[axis, pl.ds(b, 1), :] = knots[after // 2, pl.ds(3 * (after % 2) + axis, 1), :]
        return carry

    lax.fori_loop(0, NBLK, place, 0)
    lane = lax.broadcasted_iota(I32, (NBLK, 128), 1)
    at = lane + shift[...]
    wrapped = at & 127
    got = []
    for axis in range(3):
        a = jnp.take_along_axis(near[axis], wrapped, axis=1, mode="promise_in_bounds")
        b = jnp.take_along_axis(far[axis], wrapped, axis=1, mode="promise_in_bounds")
        got.append(jnp.where(at < 128, a, b))
    out[:, :128] = jnp.where(lane < WIN, got[0], pltpu.roll(got[1], WIN, 1)).astype(BF16)
    out[:, 128:] = got[2][:, :WIN].astype(BF16)


def windows_of(win_start, knots):
    return pl.pallas_call(
        window_kernel,
        name="windows",
        out_shape=shape((NBLK, 3 * WIN), BF16),
        in_specs=[SM, VM],
        out_specs=VM,
        scratch_shapes=[
            pltpu.VMEM((3, NBLK, 128), F32),
            pltpu.VMEM((3, NBLK, 128), F32),
            pltpu.VMEM((NBLK, 128), I32),
        ],
    )(win_start, knots)


def sort_rows(cols):
    sub = lax.broadcasted_iota(I32, (8, 128), 0)
    k = 2
    while k <= ROWS:
        j = k // 2
        while j >= 1:
            if j >= 8:
                step = j // 8
                for v in range(32):
                    w = v ^ step
                    if v < w:
                        low = jnp.minimum(cols[v], cols[w])
                        high = jnp.maximum(cols[v], cols[w])
                        up = ((v * 8) & k) == 0
                        cols[v], cols[w] = (low, high) if up else (high, low)
            else:
                first = (sub & j) == 0
                for v in range(32):
                    x = cols[v]
                    if j == 4:
                        other = pltpu.roll(x, 4, 0)
                    else:
                        other = jnp.where(first, pltpu.roll(x, 8 - j, 0), pltpu.roll(x, j, 0))
                    low = jnp.minimum(x, other)
                    high = jnp.maximum(x, other)
                    if k >= 8:
                        take_low = first if ((v * 8) & k) == 0 else jnp.logical_not(first)
                    else:
                        take_low = first == ((sub & k) == 0)
                    cols[v] = jnp.where(take_low, low, high)
            j //= 2
        k *= 2
    return cols


def pick_lanes(x, idx):
    halves = []
    for h in range(2):
        at = idx[:, h * 128:(h + 1) * 128]
        near = at & 127
        a = jnp.take_along_axis(x[:, :128], near, axis=1, mode="promise_in_bounds")
        b = jnp.take_along_axis(x[:, 128:], near, axis=1, mode="promise_in_bounds")
        halves.append(jnp.where(at < 128, a, b))
    return jnp.concatenate(halves, axis=1)


def sort_kernel(inc, sk, skt, idx, inv, ps, bounds):
    ids = jnp.concatenate([inc[s, 160:192, :] for s in range(4)], axis=0)
    key = ids * 256.0 + lax.broadcasted_iota(I32, (SLOTS, ROWS), 1).astype(F32)
    kt = key.T
    skey = jnp.concatenate(sort_rows([kt[8 * v:8 * v + 8] for v in range(32)]), axis=0).astype(I32)
    star = skey >> 8
    sk[...] = star
    place = skey & 255
    hi = star >> 8
    for c in range(32):
        h = hi[8 * c:8 * c + 8]
        s = star[8 * c:8 * c + 8]
        first = jnp.min(jnp.where(s >= 0, h, NHI - HW))
        bounds[c] = jnp.minimum(first - first % 2, NHI - HW)
        bounds[32 + c] = jnp.max(jnp.where(s >= 0, h, -1))
    back = (place * 256 + lax.broadcasted_iota(I32, (ROWS, SLOTS), 0)).astype(F32)
    inv_rows = sort_rows([back[8 * v:8 * v + 8] for v in range(32)])
    inv[...] = (jnp.concatenate(inv_rows, axis=0).astype(I32) & 255).T
    start = star.T
    for h in range(2):
        skt[h] = start[:, h * 128:(h + 1) * 128]
    place_t = place.T
    idx[...] = place_t
    for q in range(5):
        p = jnp.concatenate([inc[s, q * CAP:(q + 1) * CAP, :] for s in range(4)], axis=0)
        ps[q * ROWS:(q + 1) * ROWS] = pick_lanes(p, place_t).T


def sort_slots(inc):
    return pl.pallas_call(
        sort_kernel,
        name="sort",
        out_shape=(
            shape((ROWS, SLOTS), I32),
            shape((2, 128, 128), I32),
            shape((SLOTS, ROWS), I32),
            shape((SLOTS, ROWS), I32),
            shape((5 * ROWS, SLOTS)),
            shape((64,), I32),
        ),
        in_specs=[VM],
        out_specs=(VM,) * 5 + (SM,),
    )(inc)


def scatter_kernel(bounds, core, sk, skt, idx, ps, res, mine, theirs, acc, rs, tall, oh):
    rs[...] = pick_lanes(res[...], idx[...]).T
    acc[...] = jnp.zeros_like(acc)
    rowh = (lax.broadcasted_iota(I32, (80, 128), 0) // 20).astype(F32).astype(BF16)
    lane = lax.broadcasted_iota(I32, (128, 256), 1).astype(F32).astype(BF16)
    zero = jnp.zeros((), BF16)
    one = jnp.ones((), BF16)

    def add_window(c, h_from, h0):
        at = pl.multiple_of(c * 8, 8)
        p = [ps[pl.ds(pl.multiple_of(q * ROWS + c * 8, 8), 8), :] for q in range(5)]
        r = rs[pl.ds(at, 8), :]
        terms = [p[i] * p[j] for i in range(5) for j in range(i, 5)] + [p[i] * r for i in range(5)]
        for t, v in enumerate(terms):
            big = v.astype(BF16).astype(F32)
            small = v - big
            tall[t * 8:t * 8 + 8, :] = big
            tall[192 + t * 8:192 + t * 8 + 8, :] = small
            if t < 4:
                tall[160 + t * 8:160 + t * 8 + 8, :] = big
                tall[352 + t * 8:352 + t * 8 + 8, :] = small
        lo = pltpu.roll(skt[c // 16] & 255, 128 - (c % 16) * 8, 1).astype(F32).astype(BF16)
        hi = sk[pl.ds(at, 8), :] >> 8
        rel = jnp.where(hi >= h_from, hi - h0, -1).astype(F32)
        columns = [[], []]
        for s in range(8):
            col = jnp.broadcast_to(lo[:, s:s + 1], (128, 256))
            oh[s * 128:(s + 1) * 128, :] = jnp.where(col == lane, one, zero)
            diff = jnp.broadcast_to(rel[s:s + 1, :], (80, 128)).astype(BF16) - rowh
            hit = [diff == 4.0 * j for j in range(HW // 4)]
            for part in range(2):
                five = [tall[pl.ds(192 * part + 8 * o + s, 8, stride=8), :] for o in (0, 8, 16, 4, 12)]
                t = jnp.concatenate(five + five, axis=0).astype(BF16)
                columns[part].append(jnp.concatenate([jnp.where(m, t, zero) for m in hit], axis=0))
        lhs = jnp.concatenate(columns[0] + columns[1], axis=1)
        rhs = jnp.concatenate([oh[...], oh[...]], axis=0)
        acc[pl.ds(pl.multiple_of(h0 * 20, 8), HW * 20), :] += jnp.dot(lhs, rhs, preferred_element_type=F32)

    def chunk(c, carry):
        h_low = bounds[c]
        add_window(c, h_low, h_low)

        def more(w, carry):
            h_from = h_low + w * HW
            add_window(c, h_from, jnp.minimum(h_from, NHI - HW))
            return carry

        lax.fori_loop(1, (bounds[32 + c] - h_low) // HW + 1, more, 0)
        return carry

    lax.fori_loop(0, 32, chunk, 0)
    me = core[0]
    for g in range(16):
        mine[g] = acc[pl.ds(pl.multiple_of((2 * g + me) * 40, 8), 40), :]
        theirs[g] = acc[pl.ds(pl.multiple_of((2 * g + 1 - me) * 40, 8), 40), :]


def scatter(bounds, core, sk, skt, idx, ps, res):
    return pl.pallas_call(
        scatter_kernel,
        name="scatter",
        out_shape=(shape((16, 40, 256)), shape((16, 40, 256))),
        in_specs=[SM, SM] + [VM] * 5,
        out_specs=(VM, VM),
        scratch_shapes=[
            pltpu.VMEM((NHI * 20, 256), F32),
            pltpu.VMEM((ROWS, SLOTS), F32),
            pltpu.VMEM((384, 128), F32),
            pltpu.VMEM((1024, 256), BF16),
        ],
    )(bounds, core, sk, skt, idx, ps, res)


def solve_kernel(parts, update, packed, total):
    total[...] = jnp.sum(parts[...], axis=0)

    def row(r):
        return jnp.concatenate([total[r:r + 1, :], total[20 + r:21 + r, :]], axis=0)

    entries = {}
    r = 0
    for i in range(5):
        for j in range(i, 5):
            entries[i, j] = row(r) + 1.0 if i == j else row(r)
            r += 1
    factor = {}
    for j in range(5):
        pivot = entries[j, j]
        for k in range(j):
            pivot = pivot - factor[j, k] * factor[j, k]
        factor[j, j] = jnp.sqrt(pivot)
        for i in range(j + 1, 5):
            running = entries[j, i]
            for k in range(j):
                running = running - factor[i, k] * factor[j, k]
            factor[i, j] = running / factor[j, j]
    forward = []
    for i in range(5):
        running = row(15 + i)
        for k in range(i):
            running = running - factor[i, k] * forward[k]
        forward.append(running / factor[i, i])
    answer = [None] * 5
    for i in reversed(range(5)):
        running = forward[i]
        for k in range(i + 1, 5):
            running = running - factor[k, i] * answer[k]
        answer[i] = running / factor[i, i]
    packed[...] = jnp.zeros_like(packed)
    for i in range(5):
        for a in range(2):
            update[i:i + 1, a * 256:(a + 1) * 256] = answer[i][a:a + 1]
            packed[8 * a + i:8 * a + i + 1, :] = answer[i][a:a + 1]


def solve(parts):
    return pl.pallas_call(
        solve_kernel,
        name="solve",
        out_shape=(shape((5, STAR_DEV)), shape((16, 256))),
        in_specs=[VM],
        out_specs=(VM, VM),
        scratch_shapes=[pltpu.VMEM((40, 256), F32)],
    )(parts)


def fit_kernel(bounds, sk, inv, ps, res, table, out, fit):
    def look_up(c, h0, found):
        star = sk[pl.ds(pl.multiple_of(c * 8, 8), 8), :]
        at = star & 127
        rel = (star >> 7) - 2 * h0
        found = list(found)
        for k in range(2 * HW):
            hit = rel == k
            for q in range(5):
                row = table[h0 + k // 2, q:q + 1, (k % 2) * 128:(k % 2) * 128 + 128]
                value = jnp.take_along_axis(
                    jnp.broadcast_to(row, (8, 128)), at, axis=1, mode="promise_in_bounds"
                )
                found[q] = jnp.where(hit, value, found[q])
        return tuple(found)

    def chunk(c, carry):
        h_low = bounds[c]
        found = look_up(c, h_low, (jnp.zeros((8, 128), F32),) * 5)

        def more(w, found):
            return look_up(c, jnp.minimum(h_low + w * HW, NHI - HW), found)

        found = lax.fori_loop(1, (bounds[32 + c] - h_low) // HW + 1, more, found)
        total = jnp.zeros((8, 128), F32)
        for q in range(5):
            total = total + ps[pl.ds(pl.multiple_of(q * ROWS + c * 8, 8), 8), :] * found[q]
        fit[pl.ds(pl.multiple_of(c * 8, 8), 8), :] = total
        return carry

    lax.fori_loop(0, 32, chunk, 0)
    out[...] = res[...] - pick_lanes(fit[...].T, inv[...])


def apply_fit(bounds, sk, inv, ps, res, table):
    return pl.pallas_call(
        fit_kernel,
        name="fit",
        out_shape=shape((SLOTS, ROWS)),
        in_specs=[SM] + [VM] * 5,
        out_specs=VM,
        scratch_shapes=[pltpu.VMEM((ROWS, SLOTS), F32)],
    )(bounds, sk, inv, ps, res, table)


def local(attitude, win_start, design, obs_value, star_design, star_local, block_dest, block_count):
    tm = lax.axis_size("tm")
    core = (lax.axis_index("tm") % 2).astype(I32)
    swap = [(i, i ^ 1) for i in range(tm)]
    chips = [list(range(0, tm, 2)), list(range(1, tm, 2))]

    outgoing, slots = pack(block_dest, block_count, star_design.transpose(1, 0, 2), star_local)
    incoming = lax.all_to_all(outgoing, "sky", 0, 0, tiled=True)

    piece = attitude.astype(F32).reshape(3, 2, 128).transpose(1, 0, 2).reshape(6, 128)
    piece = jnp.pad(piece, ((0, 2), (0, 0)))
    knots = lax.all_to_all(jnp.broadcast_to(piece[None], (tm, 8, 128)), "tm", 0, 0, tiled=True)
    windows = windows_of(win_start, knots)
    fitted = jnp.einsum("brc,bc->br", design, windows, preferred_element_type=F32)
    residual = obs_value - fitted
    out_res = spread(slots, block_count, residual)
    in_res = lax.all_to_all(out_res.reshape(4, CAP, ROWS), "sky", 0, 0, tiled=True).reshape(SLOTS, ROWS)

    sk, skt, idx, inv, ps, bounds = sort_slots(incoming)
    mine, theirs = scatter(bounds, core[None], sk, skt, idx, ps, in_res)
    pair_sum = mine + lax.ppermute(theirs, "tm", swap)
    parts = lax.all_to_all(pair_sum, "tm", 0, 0, tiled=True, axis_index_groups=chips)
    own_update, packed = solve(parts)
    other = lax.ppermute(packed, "tm", swap)
    both = jnp.where(core == 0, jnp.stack([packed, other]), jnp.stack([other, packed]))
    table = lax.all_to_all(
        jnp.broadcast_to(both[None], (16, 2, 16, 256)), "tm", 0, 0, tiled=True, axis_index_groups=chips
    ).reshape(NHI, 8, 256)
    updated = apply_fit(bounds, sk, inv, ps, in_res, table)
    returned = lax.all_to_all(updated.reshape(4, CAP, ROWS), "sky", 0, 0, tiled=True).reshape(SLOTS, ROWS)
    result = collect(slots, block_count, returned)
    return (result, own_update)


def solution(mesh):
    placed = (
        P(None, "tm"),
        P(("sky", "tm")),
        P(("sky", "tm"), None, None),
        P(("sky", "tm"), None),
        P(("sky", "tm"), None, None),
        P(("sky", "tm"), None),
        P(("sky", "tm")),
        P(("sky", "tm")),
    )
    return jax.shard_map(
        local,
        mesh=mesh,
        in_specs=placed,
        out_specs=(P(("sky", "tm"), None), P(None, ("sky", "tm"))),
        check_vma=False,
    )
```

```python
import jax
import jax.numpy as jnp
from jax import lax
from jax.experimental import pallas as pl
from jax.experimental.pallas import tpu as pltpu
from jax.sharding import PartitionSpec as P


ROWS = 256
WIN = 64
CAP = 32
NBLK = 64
SLOTS = 128
STAR_DEV = 512
PAIR = 8
HW = 16
NHI = 64
F32 = jnp.float32
BF16 = jnp.bfloat16
I32 = jnp.int32
VM = pl.BlockSpec(memory_space=pltpu.VMEM)
SM = pl.BlockSpec(memory_space=pltpu.SMEM)


def shape(dims, dtype=F32):
    return jax.ShapeDtypeStruct(dims, dtype)


def pack_kernel(sky, dest, count, partials, stars, out0, out1, out2, out3, slots, out, used):
    out[...] = jnp.zeros_like(out)
    out[:, 160:192, :] = jnp.full((4, 32, ROWS), -1.0, F32)
    for g in range(4):
        used[g] = 0

    def place(b, carry):
        g = (dest[b] - sky[0]) & 3
        k = used[g]
        used[g] = k + 1
        slots[b] = g * CAP + k
        for q in range(5):
            out[g, pl.ds(q * CAP + k, 1), :] = partials[q, pl.ds(b, 1), :]
        out[g, pl.ds(5 * CAP + k, 1), :] = stars[pl.ds(b, 1), :].astype(F32)
        return carry

    lax.fori_loop(0, count[0], place, 0)

    def skip(b, carry):
        slots[b] = -1
        return carry

    lax.fori_loop(count[0], NBLK, skip, 0)
    for d, ref in enumerate((out0, out1, out2, out3)):
        ref[...] = out[d]


def pack(sky, dest, count, partials, stars):
    *slabs, slots = pl.pallas_call(
        pack_kernel,
        name="pack",
        out_shape=(shape((192, ROWS)),) * 4 + (shape((NBLK,), I32),),
        in_specs=[SM, SM, SM, VM, VM],
        out_specs=(VM,) * 4 + (SM,),
        scratch_shapes=[pltpu.VMEM((4, 192, ROWS), F32), pltpu.SMEM((4,), I32)],
    )(sky, dest, count, partials, stars)
    return slabs, slots


def collect_kernel(slots, count, rows0, rows1, rows2, rows3, out, rows):
    out[...] = jnp.zeros_like(out)
    for d, ref in enumerate((rows0, rows1, rows2, rows3)):
        rows[d * CAP:(d + 1) * CAP] = ref[...]

    def place(b, carry):
        out[pl.ds(b, 1), :] = rows[pl.ds(slots[b], 1), :]
        return carry

    lax.fori_loop(0, count[0], place, 0)


def collect(slots, count, slabs):
    return pl.pallas_call(
        collect_kernel,
        name="collect",
        out_shape=shape((NBLK, ROWS)),
        in_specs=[SM, SM] + [VM] * 4,
        out_specs=VM,
        scratch_shapes=[pltpu.VMEM((SLOTS, ROWS), F32)],
    )(slots, count, *slabs)


STEP = 16


def residual_kernel(
    start, tiles, slots, count, knots, obs, design, out0, out1, out2, out3, near, far, shift, win, res, out
):
    step = pl.program_id(0)

    @pl.when(step == 0)
    def _():
        def place(b, carry):
            tile = tiles[b]
            after = jnp.minimum(tile + 1, 63)
            shift[pl.ds(b, 1), :] = jnp.full((1, 128), start[b] % 128, I32)
            for axis in range(3):
                near[axis, pl.ds(b, 1), :] = knots[tile // 2, pl.ds(3 * (tile % 2) + axis, 1), :]
                far[axis, pl.ds(b, 1), :] = knots[after // 2, pl.ds(3 * (after % 2) + axis, 1), :]
            return carry

        lax.fori_loop(0, NBLK, place, 0, unroll=4)
        lane = lax.broadcasted_iota(I32, (NBLK, 128), 1)
        at = lane + shift[...]
        wrapped = at & 127
        got = []
        for axis in range(3):
            a = jnp.take_along_axis(near[axis], wrapped, axis=1, mode="promise_in_bounds")
            b = jnp.take_along_axis(far[axis], wrapped, axis=1, mode="promise_in_bounds")
            got.append(jnp.where(at < 128, a, b))
        win[:, :128] = jnp.where(lane < WIN, got[0], pltpu.roll(got[1], WIN, 1)).astype(BF16)
        win[:, 128:] = got[2][:, :WIN].astype(BF16)

    at = pl.multiple_of(step * STEP, STEP)
    group = win[pl.ds(at, STEP), :]
    rows = [jnp.dot(group, design[u], preferred_element_type=F32)[u:u + 1] for u in range(STEP)]
    res[pl.ds(at, STEP), :] = obs[pl.ds(at, STEP), :] - jnp.concatenate(rows, axis=0)

    @pl.when(step == NBLK // STEP - 1)
    def _():
        out[...] = jnp.zeros_like(out)

        def place(b, carry):
            out[pl.ds(slots[b], 1), :] = res[pl.ds(b, 1), :]
            return carry

        lax.fori_loop(0, count[0], place, 0)
        for d, ref in enumerate((out0, out1, out2, out3)):
            ref[...] = out[d * CAP:(d + 1) * CAP]


def residuals(start, tiles, slots, count, knots, obs, design):
    return pl.pallas_call(
        residual_kernel,
        name="residuals",
        grid=(NBLK // STEP,),
        out_shape=(shape((CAP, ROWS)),) * 4,
        in_specs=[
            SM,
            SM,
            SM,
            SM,
            pl.BlockSpec((32, 8, 128), lambda i: (0, 0, 0)),
            pl.BlockSpec((NBLK, ROWS), lambda i: (0, 0)),
            pl.BlockSpec((STEP, 3 * WIN, ROWS), lambda i: (i, 0, 0)),
        ],
        out_specs=(pl.BlockSpec((CAP, ROWS), lambda i: (0, 0)),) * 4,
        scratch_shapes=[
            pltpu.VMEM((3, NBLK, 128), F32),
            pltpu.VMEM((3, NBLK, 128), F32),
            pltpu.VMEM((NBLK, 128), I32),
            pltpu.VMEM((NBLK, 3 * WIN), BF16),
            pltpu.VMEM((NBLK, ROWS), F32),
            pltpu.VMEM((SLOTS, ROWS), F32),
        ],
    )(start, tiles, slots, count, knots, obs, design)


def sort_rows(cols):
    sub = lax.broadcasted_iota(I32, (8, 128), 0)
    k = 2
    while k <= ROWS:
        j = k // 2
        while j >= 1:
            if j >= 8:
                step = j // 8
                for v in range(32):
                    w = v ^ step
                    if v < w:
                        low = jnp.minimum(cols[v], cols[w])
                        high = jnp.maximum(cols[v], cols[w])
                        up = ((v * 8) & k) == 0
                        cols[v], cols[w] = (low, high) if up else (high, low)
            else:
                first = (sub & j) == 0
                for v in range(32):
                    x = cols[v]
                    if j == 4:
                        other = pltpu.roll(x, 4, 0)
                    else:
                        other = jnp.where(first, pltpu.roll(x, 8 - j, 0), pltpu.roll(x, j, 0))
                    low = jnp.minimum(x, other)
                    high = jnp.maximum(x, other)
                    if k >= 8:
                        take_low = first if ((v * 8) & k) == 0 else jnp.logical_not(first)
                    else:
                        take_low = first == ((sub & k) == 0)
                    cols[v] = jnp.where(take_low, low, high)
            j //= 2
        k *= 2
    return cols


def pick_lanes(x, idx):
    halves = []
    for h in range(2):
        at = idx[:, h * 128:(h + 1) * 128]
        near = at & 127
        a = jnp.take_along_axis(x[:, :128], near, axis=1, mode="promise_in_bounds")
        b = jnp.take_along_axis(x[:, 128:], near, axis=1, mode="promise_in_bounds")
        halves.append(jnp.where(at < 128, a, b))
    return jnp.concatenate(halves, axis=1)


def sort_kernel(inc0, inc1, inc2, inc3, sk, skt, idx, inv, ps, bounds):
    inc = (inc0, inc1, inc2, inc3)
    ids = jnp.concatenate([ref[160:192, :] for ref in inc], axis=0)
    key = ids * 256.0 + lax.broadcasted_iota(I32, (SLOTS, ROWS), 1).astype(F32)
    kt = key.T
    skey = jnp.concatenate(sort_rows([kt[8 * v:8 * v + 8] for v in range(32)]), axis=0).astype(I32)
    star = skey >> 8
    sk[...] = star
    place = skey & 255
    hi = star >> 8
    wide = 0
    for c in range(32):
        h = hi[8 * c:8 * c + 8]
        s = star[8 * c:8 * c + 8]
        first = jnp.min(jnp.where(s >= 0, h, NHI - HW))
        first = jnp.minimum(first - first % 2, NHI - HW)
        last = jnp.max(jnp.where(s >= 0, h, -1))
        bounds[c] = first
        bounds[32 + c] = last
        wide = jnp.maximum(wide, last - first)
    bounds[64] = jnp.where(wide >= HW, 32, 0)
    back = (place * 256 + lax.broadcasted_iota(I32, (ROWS, SLOTS), 0)).astype(F32)
    inv_rows = sort_rows([back[8 * v:8 * v + 8] for v in range(32)])
    inv[...] = (jnp.concatenate(inv_rows, axis=0).astype(I32) & 255).T
    start = star.T
    for h in range(2):
        skt[h] = start[:, h * 128:(h + 1) * 128]
    place_t = place.T
    idx[...] = place_t
    for q in range(5):
        p = jnp.concatenate([ref[q * CAP:(q + 1) * CAP, :] for ref in inc], axis=0)
        ps[q * ROWS:(q + 1) * ROWS] = pick_lanes(p, place_t).T


def sort_slots(slabs):
    return pl.pallas_call(
        sort_kernel,
        name="sort",
        out_shape=(
            shape((ROWS, SLOTS), I32),
            shape((2, 128, 128), I32),
            shape((SLOTS, ROWS), I32),
            shape((SLOTS, ROWS), I32),
            shape((5 * ROWS, SLOTS)),
            shape((65,), I32),
        ),
        in_specs=[VM] * 4,
        out_specs=(VM,) * 5 + (SM,),
    )(*slabs)


def stacked(*refs):
    return jnp.concatenate([ref[...] for ref in refs], axis=0)


def scatter_kernel(
    bounds, core, sk, skt, idx, ps, res0, res1, res2, res3, mine, theirs, acc, rs, tall, oh
):
    rs[...] = pick_lanes(stacked(res0, res1, res2, res3), idx[...]).T
    acc[...] = jnp.zeros_like(acc)
    rowh = (lax.broadcasted_iota(I32, (80, 128), 0) // 20).astype(F32).astype(BF16)
    lane = lax.broadcasted_iota(I32, (128, 256), 1).astype(F32).astype(BF16)
    zero = jnp.zeros((), BF16)
    one = jnp.ones((), BF16)

    def add_window(c, h_from, h0, tall, oh):
        at = pl.multiple_of(c * 8, 8)
        p = [ps[pl.ds(pl.multiple_of(q * ROWS + c * 8, 8), 8), :] for q in range(5)]
        r = rs[pl.ds(at, 8), :]
        terms = [p[i] * p[j] for i in range(5) for j in range(i, 5)] + [p[i] * r for i in range(5)]
        for t, v in enumerate(terms):
            big = v.astype(BF16).astype(F32)
            small = v - big
            tall[t * 8:t * 8 + 8, :] = big
            tall[192 + t * 8:192 + t * 8 + 8, :] = small
            if t < 4:
                tall[160 + t * 8:160 + t * 8 + 8, :] = big
                tall[352 + t * 8:352 + t * 8 + 8, :] = small
        lo = pltpu.roll(skt[c // 16] & 255, 128 - (c % 16) * 8, 1).astype(F32).astype(BF16)
        hi = sk[pl.ds(at, 8), :] >> 8
        rel = jnp.where(hi >= h_from, hi - h0, -1).astype(F32)
        columns = []
        for s in range(8):
            col = jnp.broadcast_to(lo[:, s:s + 1], (128, 256))
            oh[s * 128:(s + 1) * 128, :] = jnp.where(col == lane, one, zero)
            diff = jnp.broadcast_to(rel[s:s + 1, :], (80, 128)).astype(BF16) - rowh
            hit = [diff == 4.0 * j for j in range(HW // 4)]
            both = []
            for part in range(2):
                five = [tall[pl.ds(192 * part + 8 * o + s, 8, stride=8), :] for o in (0, 8, 16, 4, 12)]
                t = jnp.concatenate(five + five, axis=0).astype(BF16)
                both += [jnp.where(m, t, zero) for m in hit]
            columns.append(jnp.concatenate(both, axis=0))
        prod = jnp.dot(jnp.concatenate(columns, axis=1), oh[...], preferred_element_type=F32)
        acc[pl.ds(pl.multiple_of(h0 * 20, 8), HW * 20), :] += prod[:HW * 20] + prod[HW * 20:]

    def chunks(n, carry):
        for u in range(PAIR):
            c = n * PAIR + u
            add_window(c, bounds[c], bounds[c], tall.at[u], oh.at[u])
        return carry

    lax.fori_loop(0, 32 // PAIR, chunks, 0)

    def rest(c, carry):
        def more(w, carry):
            h_from = bounds[c] + w * HW
            add_window(c, h_from, jnp.minimum(h_from, NHI - HW), tall.at[0], oh.at[0])
            return carry

        lax.fori_loop(1, (bounds[32 + c] - bounds[c]) // HW + 1, more, 0)
        return carry

    lax.fori_loop(0, bounds[64], rest, 0)
    me = core[0]
    for g in range(16):
        mine[g] = acc[pl.ds(pl.multiple_of((2 * g + me) * 40, 8), 40), :]
        theirs[g] = acc[pl.ds(pl.multiple_of((2 * g + 1 - me) * 40, 8), 40), :]


def scatter(bounds, core, sk, skt, idx, ps, res):
    return pl.pallas_call(
        scatter_kernel,
        name="scatter",
        out_shape=(shape((16, 40, 256)), shape((16, 40, 256))),
        in_specs=[SM, SM] + [VM] * 8,
        out_specs=(VM, VM),
        scratch_shapes=[
            pltpu.VMEM((NHI * 20, 256), F32),
            pltpu.VMEM((ROWS, SLOTS), F32),
            pltpu.VMEM((PAIR, 384, 128), F32),
            pltpu.VMEM((PAIR, 1024, 256), BF16),
        ],
    )(bounds, core, sk, skt, idx, ps, *res)


def solve_kernel(parts, update, packed, total):
    total[...] = jnp.sum(parts[...], axis=0)

    def row(r):
        return jnp.concatenate([total[r:r + 1, :], total[20 + r:21 + r, :]], axis=0)

    entries = {}
    r = 0
    for i in range(5):
        for j in range(i, 5):
            entries[i, j] = row(r) + 1.0 if i == j else row(r)
            r += 1
    factor = {}
    for j in range(5):
        pivot = entries[j, j]
        for k in range(j):
            pivot = pivot - factor[j, k] * factor[j, k]
        factor[j, j] = jnp.sqrt(pivot)
        for i in range(j + 1, 5):
            running = entries[j, i]
            for k in range(j):
                running = running - factor[i, k] * factor[j, k]
            factor[i, j] = running / factor[j, j]
    forward = []
    for i in range(5):
        running = row(15 + i)
        for k in range(i):
            running = running - factor[i, k] * forward[k]
        forward.append(running / factor[i, i])
    answer = [None] * 5
    for i in reversed(range(5)):
        running = forward[i]
        for k in range(i + 1, 5):
            running = running - factor[k, i] * answer[k]
        answer[i] = running / factor[i, i]
    packed[...] = jnp.zeros_like(packed)
    for i in range(5):
        for a in range(2):
            update[i:i + 1, a * 256:(a + 1) * 256] = answer[i][a:a + 1]
            packed[8 * a + i:8 * a + i + 1, :] = answer[i][a:a + 1]


def solve(parts):
    return pl.pallas_call(
        solve_kernel,
        name="solve",
        out_shape=(shape((5, STAR_DEV)), shape((16, 256))),
        in_specs=[VM],
        out_specs=(VM, VM),
        scratch_shapes=[pltpu.VMEM((40, 256), F32)],
    )(parts)


def fit_kernel(bounds, sk, inv, ps, table, res0, res1, res2, res3, out0, out1, out2, out3, fit):
    def look_up(c, h_from, h0):
        star = sk[pl.ds(pl.multiple_of(c * 8, 8), 8), :]
        at = star & 127
        rel = jnp.where(star >= h_from * 256, (star >> 7) - 2 * h0, -1)
        found = [jnp.zeros((8, 128), F32)] * 5
        for k in range(2 * HW):
            hit = rel == k
            for q in range(5):
                row = table[h0 + k // 2, q:q + 1, (k % 2) * 128:(k % 2) * 128 + 128]
                value = jnp.take_along_axis(
                    jnp.broadcast_to(row, (8, 128)), at, axis=1, mode="promise_in_bounds"
                )
                found[q] = jnp.where(hit, value, found[q])
        total = ps[pl.ds(pl.multiple_of(c * 8, 8), 8), :] * found[0]
        for q in range(1, 5):
            total = total + ps[pl.ds(pl.multiple_of(q * ROWS + c * 8, 8), 8), :] * found[q]
        return total

    def chunks(n, carry):
        for u in range(PAIR):
            c = n * PAIR + u
            fit[pl.ds(pl.multiple_of(c * 8, 8), 8), :] = look_up(c, bounds[c], bounds[c])
        return carry

    lax.fori_loop(0, 32 // PAIR, chunks, 0)

    def rest(c, carry):
        def more(w, carry):
            h_from = bounds[c] + w * HW
            fit[pl.ds(pl.multiple_of(c * 8, 8), 8), :] += look_up(c, h_from, jnp.minimum(h_from, NHI - HW))
            return carry

        lax.fori_loop(1, (bounds[32 + c] - bounds[c]) // HW + 1, more, 0)
        return carry

    lax.fori_loop(0, bounds[64], rest, 0)
    total = stacked(res0, res1, res2, res3) - pick_lanes(fit[...].T, inv[...])
    for d, ref in enumerate((out0, out1, out2, out3)):
        ref[...] = total[d * CAP:(d + 1) * CAP]


def apply_fit(bounds, sk, inv, ps, table, res):
    return pl.pallas_call(
        fit_kernel,
        name="fit",
        out_shape=(shape((CAP, ROWS)),) * 4,
        in_specs=[SM] + [VM] * 8,
        out_specs=(VM,) * 4,
        scratch_shapes=[pltpu.VMEM((ROWS, SLOTS), F32)],
    )(bounds, sk, inv, ps, table, *res)


def to_sky(slabs, sign):
    n = lax.axis_size("sky")
    moved = {
        d: lax.ppermute(slabs[d], "sky", [(i, (i + sign * d) % n) for i in range(n)]) for d in (2, 1, 3)
    }
    return [slabs[0]] + [moved[d] for d in (1, 2, 3)]


def steps(attitude, win_start, design, obs_value, star_design, star_local, block_dest, block_count):
    tm = lax.axis_size("tm")
    core = (lax.axis_index("tm") % 2).astype(I32)
    swap = [(i, i ^ 1) for i in range(tm)]
    chips = [list(range(0, tm, 2)), list(range(1, tm, 2))]

    sky = lax.axis_index("sky").astype(I32)[None]
    outgoing, slots = pack(sky, block_dest, block_count, star_design.transpose(1, 0, 2), star_local)
    incoming = to_sky(outgoing, 1)

    piece = attitude.astype(F32).reshape(3, 2, 128).transpose(1, 0, 2).reshape(6, 128)
    piece = jnp.pad(piece, ((0, 2), (0, 0)))
    knots = lax.all_to_all(jnp.broadcast_to(piece[None], (tm, 8, 128)), "tm", 0, 0, tiled=True)
    tiles = win_start >> 7
    out_res = residuals(win_start, tiles, slots, block_count, knots, obs_value, design.transpose(0, 2, 1))
    in_res = to_sky(out_res, 1)

    sk, skt, idx, inv, ps, bounds = sort_slots(incoming)
    mine, theirs = scatter(bounds, core[None], sk, skt, idx, ps, in_res)
    pair_sum = mine + lax.ppermute(theirs, "tm", swap)
    parts = lax.all_to_all(pair_sum, "tm", 0, 0, tiled=True, axis_index_groups=chips)
    own_update, packed = solve(parts)
    other = lax.ppermute(packed, "tm", swap)
    both = jnp.where(core == 0, jnp.stack([packed, other]), jnp.stack([other, packed]))
    table = lax.all_to_all(
        jnp.broadcast_to(both[None], (16, 2, 16, 256)), "tm", 0, 0, tiled=True, axis_index_groups=chips
    ).reshape(NHI, 8, 256)
    updated = apply_fit(bounds, sk, inv, ps, table, in_res)
    returned = to_sky(updated, -1)
    result = collect(slots, block_count, returned)
    return (result, own_update)


def solution(mesh):
    placed = (
        P(None, "tm"),
        P(("sky", "tm")),
        P(("sky", "tm"), None, None),
        P(("sky", "tm"), None),
        P(("sky", "tm"), None, None),
        P(("sky", "tm"), None),
        P(("sky", "tm")),
        P(("sky", "tm")),
    )
    return jax.shard_map(
        steps,
        mesh=mesh,
        in_specs=placed,
        out_specs=(P(("sky", "tm"), None), P(None, ("sky", "tm"))),
        check_vma=False,
    )
```

```python
import jax
import jax.numpy as jnp
from jax import lax
from jax.experimental import pallas as pl
from jax.experimental.pallas import tpu as pltpu
from jax.sharding import PartitionSpec as P


ROWS = 256
WIN = 64
CAP = 32
NBLK = 64
SLOTS = 128
STAR_DEV = 512
PAIR = 8
HW = 12
NHI = 64
F32 = jnp.float32
BF16 = jnp.bfloat16
I32 = jnp.int32
VM = pl.BlockSpec(memory_space=pltpu.VMEM)
SM = pl.BlockSpec(memory_space=pltpu.SMEM)


def shape(dims, dtype=F32):
    return jax.ShapeDtypeStruct(dims, dtype)


def pack_kernel(sky, dest, count, partials, stars, out0, out1, out2, out3, slots, out, used):
    out[...] = jnp.zeros_like(out)
    out[:, 160:192, :] = lax.broadcasted_iota(I32, (4, 32, ROWS), 2).astype(F32) * (NHI * 256 // ROWS)
    for g in range(4):
        used[g] = 0

    def place(b, carry):
        g = (dest[b] - sky[0]) & 3
        k = used[g]
        used[g] = k + 1
        slots[b] = g * CAP + k
        for q in range(5):
            out[g, pl.ds(q * CAP + k, 1), :] = partials[q, pl.ds(b, 1), :]
        out[g, pl.ds(5 * CAP + k, 1), :] = stars[pl.ds(b, 1), :].astype(F32)
        return carry

    lax.fori_loop(0, count[0], place, 0)

    def skip(b, carry):
        slots[b] = -1
        return carry

    lax.fori_loop(count[0], NBLK, skip, 0)
    for d, ref in enumerate((out0, out1, out2, out3)):
        ref[...] = out[d]


def pack(sky, dest, count, partials, stars):
    *slabs, slots = pl.pallas_call(
        pack_kernel,
        name="pack",
        out_shape=(shape((192, ROWS)),) * 4 + (shape((NBLK,), I32),),
        in_specs=[SM, SM, SM, VM, VM],
        out_specs=(VM,) * 4 + (SM,),
        scratch_shapes=[pltpu.VMEM((4, 192, ROWS), F32), pltpu.SMEM((4,), I32)],
    )(sky, dest, count, partials, stars)
    return slabs, slots


def collect_kernel(slots, count, rows0, rows1, rows2, rows3, out, rows):
    out[...] = jnp.zeros_like(out)
    for d, ref in enumerate((rows0, rows1, rows2, rows3)):
        rows[d * CAP:(d + 1) * CAP] = ref[...]

    def place(b, carry):
        out[pl.ds(b, 1), :] = rows[pl.ds(slots[b], 1), :]
        return carry

    lax.fori_loop(0, count[0], place, 0)


def collect(slots, count, slabs):
    return pl.pallas_call(
        collect_kernel,
        name="collect",
        out_shape=shape((NBLK, ROWS)),
        in_specs=[SM, SM] + [VM] * 4,
        out_specs=VM,
        scratch_shapes=[pltpu.VMEM((SLOTS, ROWS), F32)],
    )(slots, count, *slabs)


def piece_kernel(attitude, out):
    values = attitude[...].astype(F32)
    rows = jnp.concatenate([values[:, :128], values[:, 128:], jnp.zeros((2, 128), F32)], axis=0)
    out[...] = jnp.broadcast_to(rows[None], out.shape)


def pieces(attitude, copies):
    return pl.pallas_call(
        piece_kernel, name="pieces", out_shape=shape((copies, 8, 128)), in_specs=[VM], out_specs=VM
    )(attitude)


STEP = 16


def residual_kernel(
    start, tiles, slots, count, knots, obs, design, out0, out1, out2, out3, near, far, shift, win, res, out
):
    step = pl.program_id(0)

    @pl.when(step == 0)
    def _():
        def place(b, carry):
            tile = tiles[b]
            after = jnp.minimum(tile + 1, 63)
            shift[pl.ds(b, 1), :] = jnp.full((1, 128), start[b] % 128, I32)
            for axis in range(3):
                near[axis, pl.ds(b, 1), :] = knots[tile // 2, pl.ds(3 * (tile % 2) + axis, 1), :]
                far[axis, pl.ds(b, 1), :] = knots[after // 2, pl.ds(3 * (after % 2) + axis, 1), :]
            return carry

        lax.fori_loop(0, NBLK, place, 0, unroll=4)
        lane = lax.broadcasted_iota(I32, (NBLK, 128), 1)
        at = lane + shift[...]
        wrapped = at & 127
        got = []
        for axis in range(3):
            a = jnp.take_along_axis(near[axis], wrapped, axis=1, mode="promise_in_bounds")
            b = jnp.take_along_axis(far[axis], wrapped, axis=1, mode="promise_in_bounds")
            got.append(jnp.where(at < 128, a, b))
        win[:, :128] = jnp.where(lane < WIN, got[0], pltpu.roll(got[1], WIN, 1)).astype(BF16)
        win[:, 128:] = got[2][:, :WIN].astype(BF16)

    at = pl.multiple_of(step * STEP, STEP)
    group = win[pl.ds(at, STEP), :]
    rows = [jnp.dot(group, design[u], preferred_element_type=F32)[u:u + 1] for u in range(STEP)]
    res[pl.ds(at, STEP), :] = obs[pl.ds(at, STEP), :] - jnp.concatenate(rows, axis=0)

    @pl.when(step == NBLK // STEP - 1)
    def _():
        out[...] = jnp.zeros_like(out)

        def place(b, carry):
            out[pl.ds(slots[b], 1), :] = res[pl.ds(b, 1), :]
            return carry

        lax.fori_loop(0, count[0], place, 0)
        for d, ref in enumerate((out0, out1, out2, out3)):
            ref[...] = out[d * CAP:(d + 1) * CAP]


def residuals(start, tiles, slots, count, knots, obs, design):
    return pl.pallas_call(
        residual_kernel,
        name="residuals",
        grid=(NBLK // STEP,),
        out_shape=(shape((CAP, ROWS)),) * 4,
        in_specs=[
            SM,
            SM,
            SM,
            SM,
            pl.BlockSpec((32, 8, 128), lambda i: (0, 0, 0)),
            pl.BlockSpec((NBLK, ROWS), lambda i: (0, 0)),
            pl.BlockSpec((STEP, 3 * WIN, ROWS), lambda i: (i, 0, 0)),
        ],
        out_specs=(pl.BlockSpec((CAP, ROWS), lambda i: (0, 0)),) * 4,
        scratch_shapes=[
            pltpu.VMEM((3, NBLK, 128), F32),
            pltpu.VMEM((3, NBLK, 128), F32),
            pltpu.VMEM((NBLK, 128), I32),
            pltpu.VMEM((NBLK, 3 * WIN), BF16),
            pltpu.VMEM((NBLK, ROWS), F32),
            pltpu.VMEM((SLOTS, ROWS), F32),
        ],
    )(start, tiles, slots, count, knots, obs, design)


def sort_rows(key):
    sub = lax.broadcasted_iota(I32, (8, 128), 0)
    left = lax.broadcasted_iota(I32, (8, 128), 1) < 64
    sign = jnp.where(left, 1.0, -1.0)
    cols = [key[8 * v:8 * v + 8] * sign for v in range(32)]
    k = 2
    while k <= 2 * ROWS:
        j = k // 2
        if k == 2 * ROWS:
            for v in range(32):
                x = cols[v] * sign
                other = pltpu.roll(x, 64, 1)
                cols[v] = jnp.where(left, jnp.minimum(x, other), jnp.maximum(x, other))
            j //= 2
        while j >= 1:
            if j >= 8:
                step = j // 8
                for v in range(32):
                    w = v ^ step
                    if v < w:
                        low = jnp.minimum(cols[v], cols[w])
                        high = jnp.maximum(cols[v], cols[w])
                        up = ((v * 8) & k) == 0
                        cols[v], cols[w] = (low, high) if up else (high, low)
            else:
                first = (sub & j) == 0
                for v in range(32):
                    x = cols[v]
                    if j == 4:
                        other = pltpu.roll(x, 4, 0)
                    else:
                        other = jnp.where(first, pltpu.roll(x, 8 - j, 0), pltpu.roll(x, j, 0))
                    low = jnp.minimum(x, other)
                    high = jnp.maximum(x, other)
                    if k >= 8:
                        take_low = first if ((v * 8) & k) == 0 else jnp.logical_not(first)
                    else:
                        take_low = first == ((sub & k) == 0)
                    cols[v] = jnp.where(take_low, low, high)
            j //= 2
        k *= 2
    return jnp.concatenate(cols, axis=0)


def pick_rows(x, rank):
    tops = []
    for top in range(2):
        halves = []
        for h in range(2):
            at = rank[64 * top:64 * top + 64, 128 * h:128 * h + 128]
            near = at & 127
            got = None
            for code in range(4):
                piece = x[64 * (code // 2):64 * (code // 2) + 64, 128 * (code % 2):128 * (code % 2) + 128]
                value = jnp.take_along_axis(piece, near, axis=1, mode="promise_in_bounds")
                got = value if code == 0 else jnp.where((at >> 7) == code, value, got)
            halves.append(got)
        tops.append(jnp.concatenate(halves, axis=1))
    return jnp.concatenate(tops, axis=0)


def to_chunks(xt):
    left = lax.broadcasted_iota(I32, (8, 128), 1) < 64
    low, high = [], []
    for n in range(16):
        a = xt[16 * n:16 * n + 8]
        b = xt[16 * n + 8:16 * n + 16]
        low.append(jnp.where(left, a, pltpu.roll(b, 64, 1)))
        high.append(jnp.where(left, pltpu.roll(a, 64, 1), b))
    return low + high


def from_chunks(chunks):
    left = lax.broadcasted_iota(I32, (8, 128), 1) < 64
    rows = []
    for n in range(16):
        low, high = chunks[n], chunks[16 + n]
        rows.append(jnp.where(left, low, pltpu.roll(high, 64, 1)))
        rows.append(jnp.where(left, pltpu.roll(low, 64, 1), high))
    return jnp.concatenate(rows, axis=0)


def sort_kernel(inc0, inc1, inc2, inc3, star, skt, rank, came, ps, bounds):
    inc = (inc0, inc1, inc2, inc3)
    ids = jnp.concatenate([ref[160:192, :] for ref in inc], axis=0)
    slot = lax.broadcasted_iota(I32, (SLOTS, ROWS), 0)
    row = lax.broadcasted_iota(I32, (SLOTS, ROWS), 1)
    key = ids * 512.0 + ((slot >> 6) * 256 + row).astype(F32)
    srt = sort_rows(key.T).astype(I32)
    ids_t = srt >> 9
    place = srt & 511
    wide = 0
    for c, piece in enumerate(to_chunks(ids_t)):
        star[c] = piece
        h = piece >> 8
        first = jnp.min(jnp.where(piece >= 0, h, NHI - HW))
        first = jnp.minimum(first - first % 2, NHI - HW)
        last = jnp.max(jnp.where(piece >= 0, h, -1))
        bounds[c] = first
        bounds[32 + c] = last
        wide = jnp.maximum(wide, last - first)
    bounds[64] = jnp.where(wide >= HW, 32, 0)
    came[...] = place
    ids_a = ids_t.T
    ahead = jnp.concatenate([ids_a[:, 8:], ids_a[:, :8]], axis=1)
    for half in range(2):
        both = jnp.concatenate([ids_a[64 * half:64 * half + 64], ahead[64 * half:64 * half + 64]], axis=0)
        for h in range(2):
            skt[2 * half + h] = both[:, 128 * h:128 * h + 128]
    rank_a = place.T
    rank[...] = rank_a
    for q in range(5):
        p = jnp.concatenate([ref[q * CAP:(q + 1) * CAP, :] for ref in inc], axis=0)
        for c, piece in enumerate(to_chunks(pick_rows(p, rank_a).T)):
            ps[q * 32 + c] = piece


def sort_slots(slabs):
    return pl.pallas_call(
        sort_kernel,
        name="sort",
        out_shape=(
            shape((32, 8, 128), I32),
            shape((4, 128, 128), I32),
            shape((SLOTS, ROWS), I32),
            shape((ROWS, SLOTS), I32),
            shape((160, 8, 128)),
            shape((65,), I32),
        ),
        in_specs=[VM] * 4,
        out_specs=(VM,) * 5 + (SM,),
    )(*slabs)


def invert_kernel(came, inv):
    slot = lax.broadcasted_iota(I32, (ROWS, SLOTS), 1)
    row = lax.broadcasted_iota(I32, (ROWS, SLOTS), 0)
    back = (came[...] * 512 + (slot >> 6) * 256 + row).astype(F32)
    inv[...] = (sort_rows(back).astype(I32) & 511).T


def invert(came):
    return pl.pallas_call(
        invert_kernel, name="invert", out_shape=shape((SLOTS, ROWS), I32), in_specs=[VM], out_specs=VM
    )(came)


def stacked(*refs):
    return jnp.concatenate([ref[...] for ref in refs], axis=0)


def scatter_kernel(
    bounds, core, star, skt, rank, ps, res0, res1, res2, res3, mine, theirs, acc, rs, tall, oh
):
    for c, piece in enumerate(to_chunks(pick_rows(stacked(res0, res1, res2, res3), rank[...]).T)):
        rs[c] = piece
    acc[...] = jnp.zeros_like(acc)
    rowh = (lax.broadcasted_iota(I32, (80, 128), 0) // 20).astype(F32).astype(BF16)
    lane = lax.broadcasted_iota(I32, (128, 256), 1).astype(F32).astype(BF16)
    zero = jnp.zeros((), BF16)
    one = jnp.ones((), BF16)

    def add_window(c, h_from, h0, tall, oh):
        p = [ps[q * 32 + c] for q in range(5)]
        r = rs[c]
        terms = [p[i] * p[j] for i in range(5) for j in range(i, 5)] + [p[i] * r for i in range(5)]
        for t, v in enumerate(terms):
            big = v.astype(BF16).astype(F32)
            small = v - big
            tall[t * 8:t * 8 + 8, :] = big
            tall[192 + t * 8:192 + t * 8 + 8, :] = small
            if t < 4:
                tall[160 + t * 8:160 + t * 8 + 8, :] = big
                tall[352 + t * 8:352 + t * 8 + 8, :] = small
        lo = pltpu.roll(skt[c // 8] & 255, 128 - (c % 8) * 16, 1).astype(F32).astype(BF16)
        hi = star[c] >> 8
        rel = jnp.where(hi >= h_from, hi - h0, -1).astype(F32)
        columns = []
        for s in range(8):
            col = jnp.broadcast_to(lo[:, s:s + 1], (128, 256))
            oh[s * 128:(s + 1) * 128, :] = jnp.where(col == lane, one, zero)
            diff = jnp.broadcast_to(rel[s:s + 1, :], (80, 128)).astype(BF16) - rowh
            hit = [diff == 4.0 * j for j in range(HW // 4)]
            both = []
            for part in range(2):
                five = [tall[pl.ds(192 * part + 8 * o + s, 8, stride=8), :] for o in (0, 8, 16, 4, 12)]
                t = jnp.concatenate(five + five, axis=0).astype(BF16)
                both += [jnp.where(m, t, zero) for m in hit]
            columns.append(jnp.concatenate(both, axis=0))
        prod = jnp.dot(jnp.concatenate(columns, axis=1), oh[...], preferred_element_type=F32)
        acc[pl.ds(pl.multiple_of(h0 * 20, 8), HW * 20), :] += prod[:HW * 20] + prod[HW * 20:]

    def chunks(n, carry):
        for u in range(PAIR):
            c = n * PAIR + u
            add_window(c, bounds[c], bounds[c], tall.at[u], oh.at[u])
        return carry

    lax.fori_loop(0, 32 // PAIR, chunks, 0)

    def rest(c, carry):
        def more(w, carry):
            h_from = bounds[c] + w * HW
            add_window(c, h_from, jnp.minimum(h_from, NHI - HW), tall.at[0], oh.at[0])
            return carry

        lax.fori_loop(1, (bounds[32 + c] - bounds[c]) // HW + 1, more, 0)
        return carry

    lax.fori_loop(0, bounds[64], rest, 0)
    me = core[0]
    for g in range(16):
        mine[g] = acc[pl.ds(pl.multiple_of((2 * g + me) * 40, 8), 40), :]
        theirs[g] = acc[pl.ds(pl.multiple_of((2 * g + 1 - me) * 40, 8), 40), :]


def scatter(bounds, core, star, skt, rank, ps, res):
    return pl.pallas_call(
        scatter_kernel,
        name="scatter",
        out_shape=(shape((16, 40, 256)), shape((16, 40, 256))),
        in_specs=[SM, SM] + [VM] * 8,
        out_specs=(VM, VM),
        scratch_shapes=[
            pltpu.VMEM((NHI * 20, 256), F32),
            pltpu.VMEM((32, 8, 128), F32),
            pltpu.VMEM((PAIR, 384, 128), F32),
            pltpu.VMEM((PAIR, 1024, 256), BF16),
        ],
    )(bounds, core, star, skt, rank, ps, *res)


def solve_kernel(parts, update, packed, total, own):
    total[...] = jnp.sum(parts[...], axis=0)

    def row(r):
        return jnp.concatenate([total[r:r + 1, :], total[20 + r:21 + r, :]], axis=0)

    entries = {}
    r = 0
    for i in range(5):
        for j in range(i, 5):
            entries[i, j] = row(r) + 1.0 if i == j else row(r)
            r += 1
    factor = {}
    for j in range(5):
        pivot = entries[j, j]
        for k in range(j):
            pivot = pivot - factor[j, k] * factor[j, k]
        factor[j, j] = jnp.sqrt(pivot)
        for i in range(j + 1, 5):
            running = entries[j, i]
            for k in range(j):
                running = running - factor[i, k] * factor[j, k]
            factor[i, j] = running / factor[j, j]
    forward = []
    for i in range(5):
        running = row(15 + i)
        for k in range(i):
            running = running - factor[i, k] * forward[k]
        forward.append(running / factor[i, i])
    answer = [None] * 5
    for i in reversed(range(5)):
        running = forward[i]
        for k in range(i + 1, 5):
            running = running - factor[k, i] * answer[k]
        answer[i] = running / factor[i, i]
    own[20:] = jnp.zeros((4, 128), F32)
    for i in range(5):
        for a in range(2):
            update[i:i + 1, a * 256:(a + 1) * 256] = answer[i][a:a + 1]
            for half in range(2):
                at = 10 * a + 5 * half + i
                own[at:at + 1, :] = answer[i][a:a + 1, 128 * half:128 * half + 128]
    packed[...] = jnp.broadcast_to(own[...][None], packed.shape)


def solve(parts):
    return pl.pallas_call(
        solve_kernel,
        name="solve",
        out_shape=(shape((5, STAR_DEV)), shape((16, 24, 128))),
        in_specs=[VM],
        out_specs=(VM, VM),
        scratch_shapes=[pltpu.VMEM((40, 256), F32), pltpu.VMEM((24, 128), F32)],
    )(parts)


def fit_kernel(
    bounds, core, star, inv, ps, near, far, res0, res1, res2, res3, out0, out1, out2, out3, table, fit
):
    for g in range(16):
        for a in range(2):
            for half in range(2):
                rows = slice(10 * a + 5 * half, 10 * a + 5 * half + 5)
                table[4 * g + 2 * core[0] + a, :5, 128 * half:128 * half + 128] = near[g, rows, :]
                table[4 * g + 2 - 2 * core[0] + a, :5, 128 * half:128 * half + 128] = far[g, rows, :]

    def look_up(c, h_from, h0):
        ids = star[c]
        at = ids & 127
        rel = jnp.where(ids >= h_from * 256, (ids >> 7) - 2 * h0, -1)
        found = [jnp.zeros((8, 128), F32)] * 5
        for k in range(2 * HW):
            hit = rel == k
            for q in range(5):
                row = table[h0 + k // 2, q:q + 1, (k % 2) * 128:(k % 2) * 128 + 128]
                value = jnp.take_along_axis(
                    jnp.broadcast_to(row, (8, 128)), at, axis=1, mode="promise_in_bounds"
                )
                found[q] = jnp.where(hit, value, found[q])
        total = ps[c] * found[0]
        for q in range(1, 5):
            total = total + ps[q * 32 + c] * found[q]
        return total

    def chunks(n, carry):
        for u in range(PAIR):
            c = n * PAIR + u
            fit[c] = look_up(c, bounds[c], bounds[c])
        return carry

    lax.fori_loop(0, 32 // PAIR, chunks, 0)

    def rest(c, carry):
        def more(w, carry):
            h_from = bounds[c] + w * HW
            fit[c] += look_up(c, h_from, jnp.minimum(h_from, NHI - HW))
            return carry

        lax.fori_loop(1, (bounds[32 + c] - bounds[c]) // HW + 1, more, 0)
        return carry

    lax.fori_loop(0, bounds[64], rest, 0)
    total = stacked(res0, res1, res2, res3) - pick_rows(from_chunks([fit[c] for c in range(32)]).T, inv[...])
    for d, ref in enumerate((out0, out1, out2, out3)):
        ref[...] = total[d * CAP:(d + 1) * CAP]


def apply_fit(bounds, core, star, inv, ps, near, far, res):
    return pl.pallas_call(
        fit_kernel,
        name="fit",
        out_shape=(shape((CAP, ROWS)),) * 4,
        in_specs=[SM, SM] + [VM] * 9,
        out_specs=(VM,) * 4,
        scratch_shapes=[pltpu.VMEM((NHI, 8, 256), F32), pltpu.VMEM((32, 8, 128), F32)],
    )(bounds, core, star, inv, ps, near, far, *res)


def to_sky(slabs, sign):
    n = lax.axis_size("sky")
    moved = {
        d: lax.ppermute(slabs[d], "sky", [(i, (i + sign * d) % n) for i in range(n)]) for d in (2, 1, 3)
    }
    return [slabs[0]] + [moved[d] for d in (1, 2, 3)]


def steps(attitude, win_start, design, obs_value, star_design, star_local, block_dest, block_count):
    tm = lax.axis_size("tm")
    core = (lax.axis_index("tm") % 2).astype(I32)
    swap = [(i, i ^ 1) for i in range(tm)]
    chips = [list(range(0, tm, 2)), list(range(1, tm, 2))]

    sky = lax.axis_index("sky").astype(I32)[None]
    outgoing, slots = pack(sky, block_dest, block_count, star_design.transpose(1, 0, 2), star_local)
    incoming = to_sky(outgoing, 1)

    knots = lax.all_to_all(pieces(attitude, tm), "tm", 0, 0, tiled=True)
    tiles = win_start >> 7
    out_res = residuals(win_start, tiles, slots, block_count, knots, obs_value, design.transpose(0, 2, 1))
    in_res = to_sky(out_res, 1)

    star, skt, rank, came, ps, bounds = sort_slots(incoming)
    mine, theirs = scatter(bounds, core[None], star, skt, rank, ps, in_res)
    pair_sum = mine + lax.ppermute(theirs, "tm", swap)
    parts = lax.all_to_all(pair_sum, "tm", 0, 0, tiled=True, axis_index_groups=chips)
    own_update, packed = solve(parts)
    near = lax.all_to_all(packed, "tm", 0, 0, tiled=True, axis_index_groups=chips)
    inv = invert(came)
    far = lax.ppermute(near, "tm", swap)
    updated = apply_fit(bounds, core[None], star, inv, ps, near, far, in_res)
    returned = to_sky(updated, -1)
    result = collect(slots, block_count, returned)
    return (result, own_update)


def solution(mesh):
    placed = (
        P(None, "tm"),
        P(("sky", "tm")),
        P(("sky", "tm"), None, None),
        P(("sky", "tm"), None),
        P(("sky", "tm"), None, None),
        P(("sky", "tm"), None),
        P(("sky", "tm")),
        P(("sky", "tm")),
    )
    return jax.shard_map(
        steps,
        mesh=mesh,
        in_specs=placed,
        out_specs=(P(("sky", "tm"), None), P(None, ("sky", "tm"))),
        check_vma=False,
    )
```

```python
import jax
import jax.numpy as jnp
from jax import lax
from jax.experimental import pallas as pl
from jax.experimental.pallas import tpu as pltpu
from jax.sharding import PartitionSpec as P


ROWS = 256
WIN = 64
CAP = 32
NBLK = 64
SLOTS = 128
STAR_DEV = 512
PAIR = 8
HW = 12
NHI = 64
F32 = jnp.float32
BF16 = jnp.bfloat16
I32 = jnp.int32
VM = pl.BlockSpec(memory_space=pltpu.VMEM)
ROOM = pltpu.CompilerParams(vmem_limit_bytes=24 << 20)
SM = pl.BlockSpec(memory_space=pltpu.SMEM)


def shape(dims, dtype=F32):
    return jax.ShapeDtypeStruct(dims, dtype)


def pack_kernel(sky, dest, count, partials, stars, out0, out1, out2, out3, slots, out, used):
    out[...] = jnp.zeros_like(out)
    out[:, 160:192, :] = lax.broadcasted_iota(I32, (4, 32, ROWS), 2).astype(F32) * (NHI * 256 // ROWS)
    for g in range(4):
        used[g] = 0

    def place(b, carry):
        g = (dest[b] - sky[0]) & 3
        k = used[g]
        used[g] = k + 1
        slots[b] = g * CAP + k
        for q in range(5):
            out[g, pl.ds(q * CAP + k, 1), :] = partials[q, pl.ds(b, 1), :]
        out[g, pl.ds(5 * CAP + k, 1), :] = stars[pl.ds(b, 1), :].astype(F32)
        return carry

    lax.fori_loop(0, count[0], place, 0)

    def skip(b, carry):
        slots[b] = -1
        return carry

    lax.fori_loop(count[0], NBLK, skip, 0)
    for d, ref in enumerate((out0, out1, out2, out3)):
        ref[...] = out[d]


def pack(sky, dest, count, partials, stars):
    *slabs, slots = pl.pallas_call(
        pack_kernel,
        name="pack",
        compiler_params=ROOM,
        out_shape=(shape((192, ROWS)),) * 4 + (shape((NBLK,), I32),),
        in_specs=[SM, SM, SM, VM, VM],
        out_specs=(VM,) * 4 + (SM,),
        scratch_shapes=[pltpu.VMEM((4, 192, ROWS), F32), pltpu.SMEM((4,), I32)],
    )(sky, dest, count, partials, stars)
    return slabs, slots


def collect_kernel(slots, count, rows0, rows1, rows2, rows3, out, rows):
    out[...] = jnp.zeros_like(out)
    for d, ref in enumerate((rows0, rows1, rows2, rows3)):
        rows[d * CAP:(d + 1) * CAP] = ref[...]

    def place(b, carry):
        out[pl.ds(b, 1), :] = rows[pl.ds(slots[b], 1), :]
        return carry

    lax.fori_loop(0, count[0], place, 0)


def collect(slots, count, slabs):
    return pl.pallas_call(
        collect_kernel,
        name="collect",
        compiler_params=ROOM,
        out_shape=shape((NBLK, ROWS)),
        in_specs=[SM, SM] + [VM] * 4,
        out_specs=VM,
        scratch_shapes=[pltpu.VMEM((SLOTS, ROWS), F32)],
    )(slots, count, *slabs)


def piece_kernel(attitude, out):
    values = attitude[...].astype(F32)
    rows = jnp.concatenate([values[:, :128], values[:, 128:], jnp.zeros((2, 128), F32)], axis=0)
    out[...] = jnp.broadcast_to(rows[None], out.shape)


def pieces(attitude, copies):
    return pl.pallas_call(
        piece_kernel, name="pieces", compiler_params=ROOM, out_shape=shape((copies, 8, 128)), in_specs=[VM], out_specs=VM
    )(attitude)


STEP = 16


def residual_kernel(
    start, tiles, slots, count, knots, obs, design, out0, out1, out2, out3, near, far, shift, win, res, out
):
    step = pl.program_id(0)

    @pl.when(step == 0)
    def _():
        def place(b, carry):
            tile = tiles[b]
            after = jnp.minimum(tile + 1, 63)
            shift[pl.ds(b, 1), :] = jnp.full((1, 128), start[b] & 127, I32)
            for axis in range(3):
                near[axis, pl.ds(b, 1), :] = knots[tile >> 1, pl.ds(3 * (tile & 1) + axis, 1), :]
                far[axis, pl.ds(b, 1), :] = knots[after >> 1, pl.ds(3 * (after & 1) + axis, 1), :]
            return carry

        lax.fori_loop(0, NBLK, place, 0, unroll=4)
        lane = lax.broadcasted_iota(I32, (NBLK, 128), 1)
        at = lane + shift[...]
        wrapped = at & 127
        got = []
        for axis in range(3):
            a = jnp.take_along_axis(near[axis], wrapped, axis=1, mode="promise_in_bounds")
            b = jnp.take_along_axis(far[axis], wrapped, axis=1, mode="promise_in_bounds")
            got.append(jnp.where(at < 128, a, b))
        win[:, :128] = jnp.where(lane < WIN, got[0], pltpu.roll(got[1], WIN, 1)).astype(BF16)
        win[:, 128:] = got[2][:, :WIN].astype(BF16)

    at = pl.multiple_of(step * STEP, STEP)
    group = win[pl.ds(at, STEP), :]
    rows = [jnp.dot(group, design[u], preferred_element_type=F32)[u:u + 1] for u in range(STEP)]
    res[pl.ds(at, STEP), :] = obs[pl.ds(at, STEP), :] - jnp.concatenate(rows, axis=0)

    @pl.when(step == NBLK // STEP - 1)
    def _():
        out[...] = jnp.zeros_like(out)

        def place(b, carry):
            out[pl.ds(slots[b], 1), :] = res[pl.ds(b, 1), :]
            return carry

        lax.fori_loop(0, count[0], place, 0)
        for d, ref in enumerate((out0, out1, out2, out3)):
            ref[...] = out[d * CAP:(d + 1) * CAP]


def residuals(start, tiles, slots, count, knots, obs, design):
    return pl.pallas_call(
        residual_kernel,
        name="residuals",
        compiler_params=ROOM,
        grid=(NBLK // STEP,),
        out_shape=(shape((CAP, ROWS)),) * 4,
        in_specs=[
            SM,
            SM,
            SM,
            SM,
            pl.BlockSpec((32, 8, 128), lambda i: (0, 0, 0)),
            pl.BlockSpec((NBLK, ROWS), lambda i: (0, 0)),
            pl.BlockSpec((STEP, 3 * WIN, ROWS), lambda i: (i, 0, 0)),
        ],
        out_specs=(pl.BlockSpec((CAP, ROWS), lambda i: (0, 0)),) * 4,
        scratch_shapes=[
            pltpu.VMEM((3, NBLK, 128), F32),
            pltpu.VMEM((3, NBLK, 128), F32),
            pltpu.VMEM((NBLK, 128), I32),
            pltpu.VMEM((NBLK, 3 * WIN), BF16),
            pltpu.VMEM((NBLK, ROWS), F32),
            pltpu.VMEM((SLOTS, ROWS), F32),
        ],
    )(start, tiles, slots, count, knots, obs, design)


def sort_rows(key):
    sub = lax.broadcasted_iota(I32, (8, 128), 0)
    left = lax.broadcasted_iota(I32, (8, 128), 1) < 64
    sign = jnp.where(left, 1.0, -1.0)
    cols = [key[8 * v:8 * v + 8] * sign for v in range(32)]
    k = 2
    while k <= 2 * ROWS:
        j = k // 2
        if k == 2 * ROWS:
            for v in range(32):
                x = cols[v] * sign
                other = pltpu.roll(x, 64, 1)
                cols[v] = jnp.where(left, jnp.minimum(x, other), jnp.maximum(x, other))
            j //= 2
        while j >= 1:
            if j >= 8:
                step = j // 8
                for v in range(32):
                    w = v ^ step
                    if v < w:
                        low = jnp.minimum(cols[v], cols[w])
                        high = jnp.maximum(cols[v], cols[w])
                        up = ((v * 8) & k) == 0
                        cols[v], cols[w] = (low, high) if up else (high, low)
            else:
                first = (sub & j) == 0
                for v in range(32):
                    x = cols[v]
                    if j == 4:
                        other = pltpu.roll(x, 4, 0)
                    else:
                        other = jnp.where(first, pltpu.roll(x, 8 - j, 0), pltpu.roll(x, j, 0))
                    low = jnp.minimum(x, other)
                    high = jnp.maximum(x, other)
                    if k >= 8:
                        take_low = first if ((v * 8) & k) == 0 else jnp.logical_not(first)
                    else:
                        take_low = first == ((sub & k) == 0)
                    cols[v] = jnp.where(take_low, low, high)
            j //= 2
        k *= 2
    return jnp.concatenate(cols, axis=0)


def pick_rows(x, rank):
    tops = []
    for top in range(2):
        halves = []
        for h in range(2):
            at = rank[64 * top:64 * top + 64, 128 * h:128 * h + 128]
            near = at & 127
            got = None
            for code in range(4):
                piece = x[64 * (code // 2):64 * (code // 2) + 64, 128 * (code % 2):128 * (code % 2) + 128]
                value = jnp.take_along_axis(piece, near, axis=1, mode="promise_in_bounds")
                got = value if code == 0 else jnp.where((at >> 7) == code, value, got)
            halves.append(got)
        tops.append(jnp.concatenate(halves, axis=1))
    return jnp.concatenate(tops, axis=0)


def to_chunks(xt):
    left = lax.broadcasted_iota(I32, (8, 128), 1) < 64
    low, high = [], []
    for n in range(16):
        a = xt[16 * n:16 * n + 8]
        b = xt[16 * n + 8:16 * n + 16]
        low.append(jnp.where(left, a, pltpu.roll(b, 64, 1)))
        high.append(jnp.where(left, pltpu.roll(a, 64, 1), b))
    return low + high


def from_chunks(chunks):
    left = lax.broadcasted_iota(I32, (8, 128), 1) < 64
    rows = []
    for n in range(16):
        low, high = chunks[n], chunks[16 + n]
        rows.append(jnp.where(left, low, pltpu.roll(high, 64, 1)))
        rows.append(jnp.where(left, pltpu.roll(low, 64, 1), high))
    return jnp.concatenate(rows, axis=0)


def sort_kernel(inc0, inc1, inc2, inc3, star, skt, rank, came, ps, bounds):
    inc = (inc0, inc1, inc2, inc3)
    ids = jnp.concatenate([ref[160:192, :] for ref in inc], axis=0)
    slot = lax.broadcasted_iota(I32, (SLOTS, ROWS), 0)
    row = lax.broadcasted_iota(I32, (SLOTS, ROWS), 1)
    key = ids * 512.0 + ((slot >> 6) * 256 + row).astype(F32)
    srt = sort_rows(key.T).astype(I32)
    ids_t = srt >> 9
    place = srt & 511
    wide = 0
    for c, piece in enumerate(to_chunks(ids_t)):
        star[c] = piece
        h = piece >> 8
        first = jnp.min(jnp.where(piece >= 0, h, NHI - HW))
        first = jnp.minimum(first - first % 2, NHI - HW)
        last = jnp.max(jnp.where(piece >= 0, h, -1))
        bounds[c] = first
        bounds[32 + c] = last
        wide = jnp.maximum(wide, last - first)
    bounds[64] = jnp.where(wide >= HW, 32, 0)
    came[...] = place
    ids_a = ids_t.T
    ahead = jnp.concatenate([ids_a[:, 8:], ids_a[:, :8]], axis=1)
    for half in range(2):
        both = jnp.concatenate([ids_a[64 * half:64 * half + 64], ahead[64 * half:64 * half + 64]], axis=0)
        for h in range(2):
            skt[2 * half + h] = both[:, 128 * h:128 * h + 128]
    rank_a = place.T
    rank[...] = rank_a
    for q in range(5):
        p = jnp.concatenate([ref[q * CAP:(q + 1) * CAP, :] for ref in inc], axis=0)
        for c, piece in enumerate(to_chunks(pick_rows(p, rank_a).T)):
            ps[q * 32 + c] = piece


def sort_slots(slabs):
    return pl.pallas_call(
        sort_kernel,
        name="sort",
        compiler_params=ROOM,
        out_shape=(
            shape((32, 8, 128), I32),
            shape((4, 128, 128), I32),
            shape((SLOTS, ROWS), I32),
            shape((ROWS, SLOTS), I32),
            shape((160, 8, 128)),
            shape((65,), I32),
        ),
        in_specs=[VM] * 4,
        out_specs=(VM,) * 5 + (SM,),
    )(*slabs)


def invert_kernel(came, inv):
    slot = lax.broadcasted_iota(I32, (ROWS, SLOTS), 1)
    row = lax.broadcasted_iota(I32, (ROWS, SLOTS), 0)
    back = (came[...] * 512 + (slot >> 6) * 256 + row).astype(F32)
    inv[...] = (sort_rows(back).astype(I32) & 511).T


def invert(came):
    return pl.pallas_call(
        invert_kernel, name="invert", compiler_params=ROOM, out_shape=shape((SLOTS, ROWS), I32), in_specs=[VM], out_specs=VM
    )(came)


def stacked(*refs):
    return jnp.concatenate([ref[...] for ref in refs], axis=0)


def scatter_kernel(
    bounds, core, star, skt, rank, ps, res0, res1, res2, res3, mine, theirs, acc, rs, tall, oh
):
    for c, piece in enumerate(to_chunks(pick_rows(stacked(res0, res1, res2, res3), rank[...]).T)):
        rs[c] = piece
    acc[...] = jnp.zeros_like(acc)
    rowh = (lax.broadcasted_iota(I32, (80, 128), 0) // 20).astype(F32).astype(BF16)
    lane = lax.broadcasted_iota(I32, (128, 256), 1).astype(F32).astype(BF16)
    zero = jnp.zeros((), BF16)
    one = jnp.ones((), BF16)

    def add_window(c, h_from, h0, tall, oh):
        p = [ps[q * 32 + c] for q in range(5)]
        r = rs[c]
        terms = [p[i] * p[j] for i in range(5) for j in range(i, 5)] + [p[i] * r for i in range(5)]
        for t, v in enumerate(terms):
            big = v.astype(BF16).astype(F32)
            small = v - big
            tall[t * 8:t * 8 + 8, :] = big
            tall[192 + t * 8:192 + t * 8 + 8, :] = small
            if t < 4:
                tall[160 + t * 8:160 + t * 8 + 8, :] = big
                tall[352 + t * 8:352 + t * 8 + 8, :] = small
        lo = pltpu.roll(skt[c // 8] & 255, 128 - (c % 8) * 16, 1).astype(F32).astype(BF16)
        hi = star[c] >> 8
        rel = jnp.where(hi >= h_from, hi - h0, -1).astype(F32)
        columns = []
        for s in range(8):
            col = jnp.broadcast_to(lo[:, s:s + 1], (128, 256))
            oh[s * 128:(s + 1) * 128, :] = jnp.where(col == lane, one, zero)
            diff = jnp.broadcast_to(rel[s:s + 1, :], (80, 128)).astype(BF16) - rowh
            hit = [diff == 4.0 * j for j in range(HW // 4)]
            both = []
            for part in range(2):
                five = [tall[pl.ds(192 * part + 8 * o + s, 8, stride=8), :] for o in (0, 8, 16, 4, 12)]
                t = jnp.concatenate(five + five, axis=0).astype(BF16)
                both += [jnp.where(m, t, zero) for m in hit]
            columns.append(jnp.concatenate(both, axis=0))
        prod = jnp.dot(jnp.concatenate(columns, axis=1), oh[...], preferred_element_type=F32)
        acc[pl.ds(pl.multiple_of(h0 * 20, 8), HW * 20), :] += prod[:HW * 20] + prod[HW * 20:]

    def chunks(n, carry):
        for u in range(PAIR):
            c = n * PAIR + u
            add_window(c, bounds[c], bounds[c], tall.at[u], oh.at[u])
        return carry

    lax.fori_loop(0, 32 // PAIR, chunks, 0)

    def rest(c, carry):
        def more(w, carry):
            h_from = bounds[c] + w * HW
            add_window(c, h_from, jnp.minimum(h_from, NHI - HW), tall.at[0], oh.at[0])
            return carry

        lax.fori_loop(1, (bounds[32 + c] - bounds[c]) // HW + 1, more, 0)
        return carry

    lax.fori_loop(0, bounds[64], rest, 0)
    me = core[0]
    for g in range(16):
        mine[g] = acc[pl.ds(pl.multiple_of((2 * g + me) * 40, 8), 40), :]
        theirs[g] = acc[pl.ds(pl.multiple_of((2 * g + 1 - me) * 40, 8), 40), :]


def scatter(bounds, core, star, skt, rank, ps, res):
    return pl.pallas_call(
        scatter_kernel,
        name="scatter",
        compiler_params=ROOM,
        out_shape=(shape((16, 40, 256)), shape((16, 40, 256))),
        in_specs=[SM, SM] + [VM] * 8,
        out_specs=(VM, VM),
        scratch_shapes=[
            pltpu.VMEM((NHI * 20, 256), F32),
            pltpu.VMEM((32, 8, 128), F32),
            pltpu.VMEM((PAIR, 384, 128), F32),
            pltpu.VMEM((PAIR, 1024, 256), BF16),
        ],
    )(bounds, core, star, skt, rank, ps, *res)


def solve_kernel(parts, update, packed, total, own):
    total[...] = jnp.sum(parts[...], axis=0)

    def row(r):
        return jnp.concatenate([total[r:r + 1, :], total[20 + r:21 + r, :]], axis=0)

    entries = {}
    r = 0
    for i in range(5):
        for j in range(i, 5):
            entries[i, j] = row(r) + 1.0 if i == j else row(r)
            r += 1
    factor = {}
    for j in range(5):
        pivot = entries[j, j]
        for k in range(j):
            pivot = pivot - factor[j, k] * factor[j, k]
        factor[j, j] = jnp.sqrt(pivot)
        for i in range(j + 1, 5):
            running = entries[j, i]
            for k in range(j):
                running = running - factor[i, k] * factor[j, k]
            factor[i, j] = running / factor[j, j]
    forward = []
    for i in range(5):
        running = row(15 + i)
        for k in range(i):
            running = running - factor[i, k] * forward[k]
        forward.append(running / factor[i, i])
    answer = [None] * 5
    for i in reversed(range(5)):
        running = forward[i]
        for k in range(i + 1, 5):
            running = running - factor[k, i] * answer[k]
        answer[i] = running / factor[i, i]
    own[20:] = jnp.zeros((4, 128), F32)
    for i in range(5):
        for a in range(2):
            update[i:i + 1, a * 256:(a + 1) * 256] = answer[i][a:a + 1]
            for half in range(2):
                at = 10 * a + 5 * half + i
                own[at:at + 1, :] = answer[i][a:a + 1, 128 * half:128 * half + 128]
    packed[...] = jnp.broadcast_to(own[...][None], packed.shape)


def solve(parts):
    return pl.pallas_call(
        solve_kernel,
        name="solve",
        compiler_params=ROOM,
        out_shape=(shape((5, STAR_DEV)), shape((16, 24, 128))),
        in_specs=[VM],
        out_specs=(VM, VM),
        scratch_shapes=[pltpu.VMEM((40, 256), F32), pltpu.VMEM((24, 128), F32)],
    )(parts)


def fit_kernel(
    bounds, core, star, inv, ps, near, far, res0, res1, res2, res3, out0, out1, out2, out3, table, fit
):
    for g in range(16):
        for a in range(2):
            for half in range(2):
                rows = slice(10 * a + 5 * half, 10 * a + 5 * half + 5)
                table[4 * g + 2 * core[0] + a, :5, 128 * half:128 * half + 128] = near[g, rows, :]
                table[4 * g + 2 - 2 * core[0] + a, :5, 128 * half:128 * half + 128] = far[g, rows, :]

    def look_up(c, h_from, h0):
        ids = star[c]
        at = ids & 127
        rel = jnp.where(ids >= h_from * 256, (ids >> 7) - 2 * h0, -1)
        found = [jnp.zeros((8, 128), F32)] * 5
        for k in range(2 * HW):
            hit = rel == k
            for q in range(5):
                row = table[h0 + k // 2, q:q + 1, (k % 2) * 128:(k % 2) * 128 + 128]
                value = jnp.take_along_axis(
                    jnp.broadcast_to(row, (8, 128)), at, axis=1, mode="promise_in_bounds"
                )
                found[q] = jnp.where(hit, value, found[q])
        total = ps[c] * found[0]
        for q in range(1, 5):
            total = total + ps[q * 32 + c] * found[q]
        return total

    def chunks(n, carry):
        for u in range(PAIR):
            c = n * PAIR + u
            fit[c] = look_up(c, bounds[c], bounds[c])
        return carry

    lax.fori_loop(0, 32 // PAIR, chunks, 0)

    def rest(c, carry):
        def more(w, carry):
            h_from = bounds[c] + w * HW
            fit[c] += look_up(c, h_from, jnp.minimum(h_from, NHI - HW))
            return carry

        lax.fori_loop(1, (bounds[32 + c] - bounds[c]) // HW + 1, more, 0)
        return carry

    lax.fori_loop(0, bounds[64], rest, 0)
    total = stacked(res0, res1, res2, res3) - pick_rows(from_chunks([fit[c] for c in range(32)]).T, inv[...])
    for d, ref in enumerate((out0, out1, out2, out3)):
        ref[...] = total[d * CAP:(d + 1) * CAP]


def apply_fit(bounds, core, star, inv, ps, near, far, res):
    return pl.pallas_call(
        fit_kernel,
        name="fit",
        compiler_params=ROOM,
        out_shape=(shape((CAP, ROWS)),) * 4,
        in_specs=[SM, SM] + [VM] * 9,
        out_specs=(VM,) * 4,
        scratch_shapes=[pltpu.VMEM((NHI, 8, 256), F32), pltpu.VMEM((32, 8, 128), F32)],
    )(bounds, core, star, inv, ps, near, far, *res)


def to_sky(slabs, sign):
    n = lax.axis_size("sky")
    moved = {
        d: lax.ppermute(slabs[d], "sky", [(i, (i + sign * d) % n) for i in range(n)]) for d in (2, 1, 3)
    }
    return [slabs[0]] + [moved[d] for d in (1, 2, 3)]


def in_hbm(x):
    return pltpu.with_memory_space_constraint(x, pltpu.HBM)


def steps(attitude, win_start, design, obs_value, star_design, star_local, block_dest, block_count):
    attitude, starts, obs_value, star_local, block_dest = map(
        in_hbm, (attitude, win_start, obs_value, star_local, block_dest)
    )
    partials = in_hbm(star_design.transpose(1, 0, 2))
    design_t = in_hbm(design.transpose(0, 2, 1))
    tm = lax.axis_size("tm")
    core = (lax.axis_index("tm") % 2).astype(I32)
    swap = [(i, i ^ 1) for i in range(tm)]
    chips = [list(range(0, tm, 2)), list(range(1, tm, 2))]

    sky = lax.axis_index("sky").astype(I32)[None]
    outgoing, slots = pack(sky, block_dest, block_count, partials, star_local)
    incoming = to_sky(outgoing, 1)

    knots = lax.all_to_all(pieces(attitude, tm), "tm", 0, 0, tiled=True)
    tiles = win_start >> 7
    out_res = residuals(starts, tiles, slots, block_count, knots, obs_value, design_t)
    in_res = to_sky(out_res, 1)

    star, skt, rank, came, ps, bounds = sort_slots(incoming)
    mine, theirs = scatter(bounds, core[None], star, skt, rank, ps, in_res)
    pair_sum = mine + lax.ppermute(theirs, "tm", swap)
    parts = lax.all_to_all(pair_sum, "tm", 0, 0, tiled=True, axis_index_groups=chips)
    own_update, packed = solve(parts)
    near = lax.all_to_all(packed, "tm", 0, 0, tiled=True, axis_index_groups=chips)
    inv = invert(came)
    far = lax.ppermute(near, "tm", swap)
    updated = apply_fit(bounds, core[None], star, inv, ps, near, far, in_res)
    returned = to_sky(updated, -1)
    result = collect(slots, block_count, returned)
    return (result, own_update)


def solution(mesh):
    placed = (
        P(None, "tm"),
        P(("sky", "tm")),
        P(("sky", "tm"), None, None),
        P(("sky", "tm"), None),
        P(("sky", "tm"), None, None),
        P(("sky", "tm"), None),
        P(("sky", "tm")),
        P(("sky", "tm")),
    )
    return jax.shard_map(
        steps,
        mesh=mesh,
        in_specs=placed,
        out_specs=(P(("sky", "tm"), None), P(None, ("sky", "tm"))),
        check_vma=False,
    )
```

```python
import jax
import jax.numpy as jnp
from jax import lax
from jax.experimental import pallas as pl
from jax.experimental.pallas import tpu as pltpu
from jax.sharding import PartitionSpec as P


ROWS = 256
WIN = 64
CAP = 32
NBLK = 64
SLOTS = 128
STAR_DEV = 512
PAIR = 16
HW = 12
NHI = 64
F32 = jnp.float32
BF16 = jnp.bfloat16
I32 = jnp.int32
VM = pl.BlockSpec(memory_space=pltpu.VMEM)
ROOM = pltpu.CompilerParams(vmem_limit_bytes=24 << 20)
SM = pl.BlockSpec(memory_space=pltpu.SMEM)


def shape(dims, dtype=F32):
    return jax.ShapeDtypeStruct(dims, dtype)


def pack_kernel(sky, dest, count, partials, stars, out0, out1, out2, out3, slots, out, used):
    out[...] = jnp.zeros_like(out)
    out[:, 160:192, :] = lax.broadcasted_iota(I32, (5, 32, ROWS), 2).astype(F32) * (NHI * 256 // ROWS)
    for g in range(4):
        used[g] = 0

    def place(b, carry):
        live = b < count[0]
        g = (dest[b] - sky[0]) & 3
        k = used[g]
        used[g] = k + live.astype(I32)
        slots[b] = jnp.where(live, g * CAP + k, -1)
        g = jnp.where(live, g, 4)
        k = jnp.where(live, k, 0)
        for q in range(5):
            out[g, pl.ds(q * CAP + k, 1), :] = partials[q, pl.ds(b, 1), :]
        out[g, pl.ds(5 * CAP + k, 1), :] = stars[pl.ds(b, 1), :].astype(F32)
        return carry

    lax.fori_loop(0, NBLK, place, 0, unroll=4)
    for d, ref in enumerate((out0, out1, out2, out3)):
        ref[...] = out[d]


def pack(sky, dest, count, partials, stars):
    *slabs, slots = pl.pallas_call(
        pack_kernel,
        name="pack",
        compiler_params=ROOM,
        out_shape=(shape((192, ROWS)),) * 4 + (shape((NBLK,), I32),),
        in_specs=[SM, SM, SM, VM, VM],
        out_specs=(VM,) * 4 + (SM,),
        scratch_shapes=[pltpu.VMEM((5, 192, ROWS), F32), pltpu.SMEM((4,), I32)],
    )(sky, dest, count, partials, stars)
    return slabs, slots


def collect_kernel(slots, count, rows0, rows1, rows2, rows3, out, rows):
    out[...] = jnp.zeros_like(out)
    for d, ref in enumerate((rows0, rows1, rows2, rows3)):
        rows[d * CAP:(d + 1) * CAP] = ref[...]

    def place(b, carry):
        out[pl.ds(b, 1), :] = rows[pl.ds(slots[b], 1), :]
        return carry

    lax.fori_loop(0, count[0], place, 0)


def collect(slots, count, slabs):
    return pl.pallas_call(
        collect_kernel,
        name="collect",
        compiler_params=ROOM,
        out_shape=shape((NBLK, ROWS)),
        in_specs=[SM, SM] + [VM] * 4,
        out_specs=VM,
        scratch_shapes=[pltpu.VMEM((SLOTS, ROWS), F32)],
    )(slots, count, *slabs)


def piece_kernel(attitude, out):
    values = attitude[...].astype(F32)
    rows = jnp.concatenate([values[:, :128], values[:, 128:], jnp.zeros((2, 128), F32)], axis=0)
    out[...] = jnp.broadcast_to(rows[None], out.shape)


def pieces(attitude, copies):
    return pl.pallas_call(
        piece_kernel, name="pieces", compiler_params=ROOM, out_shape=shape((copies, 8, 128)), in_specs=[VM], out_specs=VM
    )(attitude)


STEP = 16


def residual_kernel(
    start, slots, count, knots, obs, design, out0, out1, out2, out3, near, far, shift, win, res, out
):
    step = pl.program_id(0)

    @pl.when(step == 0)
    def _():
        def place(b, carry):
            tile = start[b] >> 7
            after = jnp.minimum(tile + 1, 63)
            shift[pl.ds(b, 1), :] = jnp.full((1, 128), start[b] & 127, I32)
            for axis in range(3):
                near[axis, pl.ds(b, 1), :] = knots[tile >> 1, pl.ds(3 * (tile & 1) + axis, 1), :]
                far[axis, pl.ds(b, 1), :] = knots[after >> 1, pl.ds(3 * (after & 1) + axis, 1), :]
            return carry

        lax.fori_loop(0, NBLK, place, 0, unroll=4)
        lane = lax.broadcasted_iota(I32, (NBLK, 128), 1)
        at = lane + shift[...]
        wrapped = at & 127
        got = []
        for axis in range(3):
            a = jnp.take_along_axis(near[axis], wrapped, axis=1, mode="promise_in_bounds")
            b = jnp.take_along_axis(far[axis], wrapped, axis=1, mode="promise_in_bounds")
            got.append(jnp.where(at < 128, a, b))
        win[:, :128] = jnp.where(lane < WIN, got[0], pltpu.roll(got[1], WIN, 1)).astype(BF16)
        win[:, 128:] = got[2][:, :WIN].astype(BF16)

    at = pl.multiple_of(step * STEP, STEP)
    group = win[pl.ds(at, STEP), :]
    rows = [jnp.dot(group, design[u], preferred_element_type=F32)[u:u + 1] for u in range(STEP)]
    res[pl.ds(at, STEP), :] = obs[pl.ds(at, STEP), :] - jnp.concatenate(rows, axis=0)

    @pl.when(step == NBLK // STEP - 1)
    def _():
        out[...] = jnp.zeros_like(out)

        def place(b, carry):
            out[pl.ds(slots[b], 1), :] = res[pl.ds(b, 1), :]
            return carry

        lax.fori_loop(0, count[0], place, 0)
        for d, ref in enumerate((out0, out1, out2, out3)):
            ref[...] = out[d * CAP:(d + 1) * CAP]


def residuals(start, slots, count, knots, obs, design):
    return pl.pallas_call(
        residual_kernel,
        name="residuals",
        compiler_params=ROOM,
        grid=(NBLK // STEP,),
        out_shape=(shape((CAP, ROWS)),) * 4,
        in_specs=[
            SM,
            SM,
            SM,
            pl.BlockSpec((32, 8, 128), lambda i: (0, 0, 0)),
            pl.BlockSpec((NBLK, ROWS), lambda i: (0, 0)),
            pl.BlockSpec((STEP, 3 * WIN, ROWS), lambda i: (i, 0, 0)),
        ],
        out_specs=(pl.BlockSpec((CAP, ROWS), lambda i: (0, 0)),) * 4,
        scratch_shapes=[
            pltpu.VMEM((3, NBLK, 128), F32),
            pltpu.VMEM((3, NBLK, 128), F32),
            pltpu.VMEM((NBLK, 128), I32),
            pltpu.VMEM((NBLK, 3 * WIN), BF16),
            pltpu.VMEM((NBLK, ROWS), F32),
            pltpu.VMEM((SLOTS, ROWS), F32),
        ],
    )(start, slots, count, knots, obs, design)


def sort_rows(key):
    sub = lax.broadcasted_iota(I32, (8, 128), 0)
    left = lax.broadcasted_iota(I32, (8, 128), 1) < 64
    sign = jnp.where(left, 1.0, -1.0)
    cols = [key[8 * v:8 * v + 8] * sign for v in range(32)]
    k = 2
    while k <= 2 * ROWS:
        j = k // 2
        if k == 2 * ROWS:
            for v in range(32):
                x = cols[v] * sign
                other = pltpu.roll(x, 64, 1)
                cols[v] = jnp.where(left, jnp.minimum(x, other), jnp.maximum(x, other))
            j //= 2
        while j >= 1:
            if j >= 8:
                step = j // 8
                for v in range(32):
                    w = v ^ step
                    if v < w:
                        low = jnp.minimum(cols[v], cols[w])
                        high = jnp.maximum(cols[v], cols[w])
                        up = ((v * 8) & k) == 0
                        cols[v], cols[w] = (low, high) if up else (high, low)
            else:
                first = (sub & j) == 0
                for v in range(32):
                    x = cols[v]
                    if j == 4:
                        other = pltpu.roll(x, 4, 0)
                    else:
                        other = jnp.where(first, pltpu.roll(x, 8 - j, 0), pltpu.roll(x, j, 0))
                    low = jnp.minimum(x, other)
                    high = jnp.maximum(x, other)
                    if k >= 8:
                        take_low = first if ((v * 8) & k) == 0 else jnp.logical_not(first)
                    else:
                        take_low = first == ((sub & k) == 0)
                    cols[v] = jnp.where(take_low, low, high)
            j //= 2
        k *= 2
    return jnp.concatenate(cols, axis=0)


def pick_rows(x, rank):
    tops = []
    for top in range(2):
        halves = []
        for h in range(2):
            at = rank[64 * top:64 * top + 64, 128 * h:128 * h + 128]
            near = at & 127
            got = None
            for code in range(4):
                piece = x[64 * (code // 2):64 * (code // 2) + 64, 128 * (code % 2):128 * (code % 2) + 128]
                value = jnp.take_along_axis(piece, near, axis=1, mode="promise_in_bounds")
                got = value if code == 0 else jnp.where((at >> 7) == code, value, got)
            halves.append(got)
        tops.append(jnp.concatenate(halves, axis=1))
    return jnp.concatenate(tops, axis=0)


def to_chunks(xt):
    left = lax.broadcasted_iota(I32, (8, 128), 1) < 64
    low, high = [], []
    for n in range(16):
        a = xt[16 * n:16 * n + 8]
        b = xt[16 * n + 8:16 * n + 16]
        low.append(jnp.where(left, a, pltpu.roll(b, 64, 1)))
        high.append(jnp.where(left, pltpu.roll(a, 64, 1), b))
    return low + high


def from_chunks(chunks):
    left = lax.broadcasted_iota(I32, (8, 128), 1) < 64
    rows = []
    for n in range(16):
        low, high = chunks[n], chunks[16 + n]
        rows.append(jnp.where(left, low, pltpu.roll(high, 64, 1)))
        rows.append(jnp.where(left, pltpu.roll(low, 64, 1), high))
    return jnp.concatenate(rows, axis=0)


def sort_kernel(inc0, inc1, inc2, inc3, star, skt, rank, came, ps, bounds):
    inc = (inc0, inc1, inc2, inc3)
    ids = jnp.concatenate([ref[160:192, :] for ref in inc], axis=0)
    slot = lax.broadcasted_iota(I32, (SLOTS, ROWS), 0)
    row = lax.broadcasted_iota(I32, (SLOTS, ROWS), 1)
    key = ids * 512.0 + ((slot >> 6) * 256 + row).astype(F32)
    srt = sort_rows(key.T).astype(I32)
    ids_t = srt >> 9
    place = srt & 511
    wide = 0
    for c, piece in enumerate(to_chunks(ids_t)):
        star[c] = piece
        h = piece >> 8
        first = jnp.min(jnp.where(piece >= 0, h, NHI - HW))
        first = jnp.minimum(first - first % 2, NHI - HW)
        last = jnp.max(jnp.where(piece >= 0, h, -1))
        bounds[c] = first
        bounds[32 + c] = last
        wide = jnp.maximum(wide, last - first)
    bounds[64] = jnp.where(wide >= HW, 32, 0)
    came[...] = place
    ids_a = ids_t.T
    ahead = jnp.concatenate([ids_a[:, 8:], ids_a[:, :8]], axis=1)
    for half in range(2):
        both = jnp.concatenate([ids_a[64 * half:64 * half + 64], ahead[64 * half:64 * half + 64]], axis=0)
        for h in range(2):
            skt[2 * half + h] = both[:, 128 * h:128 * h + 128]
    rank_a = place.T
    rank[...] = rank_a
    for q in range(5):
        p = jnp.concatenate([ref[q * CAP:(q + 1) * CAP, :] for ref in inc], axis=0)
        for c, piece in enumerate(to_chunks(pick_rows(p, rank_a).T)):
            ps[q * 32 + c] = piece


def sort_slots(slabs):
    return pl.pallas_call(
        sort_kernel,
        name="sort",
        compiler_params=ROOM,
        out_shape=(
            shape((32, 8, 128), I32),
            shape((4, 128, 128), I32),
            shape((SLOTS, ROWS), I32),
            shape((ROWS, SLOTS), I32),
            shape((160, 8, 128)),
            shape((65,), I32),
        ),
        in_specs=[VM] * 4,
        out_specs=(VM,) * 5 + (SM,),
    )(*slabs)


def invert_kernel(came, inv):
    slot = lax.broadcasted_iota(I32, (ROWS, SLOTS), 1)
    row = lax.broadcasted_iota(I32, (ROWS, SLOTS), 0)
    back = (came[...] * 512 + (slot >> 6) * 256 + row).astype(F32)
    inv[...] = (sort_rows(back).astype(I32) & 511).T


def invert(came):
    return pl.pallas_call(
        invert_kernel, name="invert", compiler_params=ROOM, out_shape=shape((SLOTS, ROWS), I32), in_specs=[VM], out_specs=VM
    )(came)


def stacked(*refs):
    return jnp.concatenate([ref[...] for ref in refs], axis=0)


def scatter_kernel(
    bounds, core, star, skt, rank, ps, res0, res1, res2, res3, mine, theirs, acc, rs, tall, oh
):
    for c, piece in enumerate(to_chunks(pick_rows(stacked(res0, res1, res2, res3), rank[...]).T)):
        rs[c] = piece
    acc[...] = jnp.zeros_like(acc)
    rowh = (lax.broadcasted_iota(I32, (80, 128), 0) // 20).astype(F32).astype(BF16)
    lane = lax.broadcasted_iota(I32, (128, 256), 1).astype(F32).astype(BF16)
    zero = jnp.zeros((), BF16)
    one = jnp.ones((), BF16)

    def add_window(c, h_from, h0, tall, oh):
        p = [ps[q * 32 + c] for q in range(5)]
        r = rs[c]
        terms = [p[i] * p[j] for i in range(5) for j in range(i, 5)] + [p[i] * r for i in range(5)]
        for t, v in enumerate(terms):
            big = v.astype(BF16).astype(F32)
            small = v - big
            tall[t * 8:t * 8 + 8, :] = big
            tall[192 + t * 8:192 + t * 8 + 8, :] = small
            if t < 4:
                tall[160 + t * 8:160 + t * 8 + 8, :] = big
                tall[352 + t * 8:352 + t * 8 + 8, :] = small
        lo = pltpu.roll(skt[c // 8] & 255, 128 - (c % 8) * 16, 1).astype(F32).astype(BF16)
        hi = star[c] >> 8
        rel = jnp.where(hi >= h_from, hi - h0, -1).astype(F32)
        columns = []
        for s in range(8):
            col = jnp.broadcast_to(lo[:, s:s + 1], (128, 256))
            oh[s * 128:(s + 1) * 128, :] = jnp.where(col == lane, one, zero)
            diff = jnp.broadcast_to(rel[s:s + 1, :], (80, 128)).astype(BF16) - rowh
            hit = [diff == 4.0 * j for j in range(HW // 4)]
            both = []
            for part in range(2):
                five = [tall[pl.ds(192 * part + 8 * o + s, 8, stride=8), :] for o in (0, 8, 16, 4, 12)]
                t = jnp.concatenate(five + five, axis=0).astype(BF16)
                both += [jnp.where(m, t, zero) for m in hit]
            columns.append(jnp.concatenate(both, axis=0))
        prod = jnp.dot(jnp.concatenate(columns, axis=1), oh[...], preferred_element_type=F32)
        acc[pl.ds(pl.multiple_of(h0 * 20, 8), HW * 20), :] += prod[:HW * 20] + prod[HW * 20:]

    def chunks(n, carry):
        for u in range(PAIR):
            c = n * PAIR + u
            add_window(c, bounds[c], bounds[c], tall.at[u], oh.at[u])
        return carry

    lax.fori_loop(0, 32 // PAIR, chunks, 0)

    def rest(c, carry):
        def more(w, carry):
            h_from = bounds[c] + w * HW
            add_window(c, h_from, jnp.minimum(h_from, NHI - HW), tall.at[0], oh.at[0])
            return carry

        lax.fori_loop(1, (bounds[32 + c] - bounds[c]) // HW + 1, more, 0)
        return carry

    lax.fori_loop(0, bounds[64], rest, 0)
    me = core[0]
    for g in range(16):
        mine[g] = acc[pl.ds(pl.multiple_of((2 * g + me) * 40, 8), 40), :]
        theirs[g] = acc[pl.ds(pl.multiple_of((2 * g + 1 - me) * 40, 8), 40), :]


def scatter(bounds, core, star, skt, rank, ps, res):
    return pl.pallas_call(
        scatter_kernel,
        name="scatter",
        compiler_params=ROOM,
        out_shape=(shape((16, 40, 256)), shape((16, 40, 256))),
        in_specs=[SM, SM] + [VM] * 8,
        out_specs=(VM, VM),
        scratch_shapes=[
            pltpu.VMEM((NHI * 20, 256), F32),
            pltpu.VMEM((32, 8, 128), F32),
            pltpu.VMEM((PAIR, 384, 128), F32),
            pltpu.VMEM((PAIR, 1024, 256), BF16),
        ],
    )(bounds, core, star, skt, rank, ps, *res)


def solve_kernel(parts, update, packed, total, own):
    total[...] = jnp.sum(parts[...], axis=0)

    def row(r):
        return jnp.concatenate([total[r:r + 1, :], total[20 + r:21 + r, :]], axis=0)

    entries = {}
    r = 0
    for i in range(5):
        for j in range(i, 5):
            entries[i, j] = row(r) + 1.0 if i == j else row(r)
            r += 1
    factor = {}
    for j in range(5):
        pivot = entries[j, j]
        for k in range(j):
            pivot = pivot - factor[j, k] * factor[j, k]
        factor[j, j] = jnp.sqrt(pivot)
        for i in range(j + 1, 5):
            running = entries[j, i]
            for k in range(j):
                running = running - factor[i, k] * factor[j, k]
            factor[i, j] = running / factor[j, j]
    forward = []
    for i in range(5):
        running = row(15 + i)
        for k in range(i):
            running = running - factor[i, k] * forward[k]
        forward.append(running / factor[i, i])
    answer = [None] * 5
    for i in reversed(range(5)):
        running = forward[i]
        for k in range(i + 1, 5):
            running = running - factor[k, i] * answer[k]
        answer[i] = running / factor[i, i]
    own[20:] = jnp.zeros((4, 128), F32)
    for i in range(5):
        for a in range(2):
            update[i:i + 1, a * 256:(a + 1) * 256] = answer[i][a:a + 1]
            for half in range(2):
                at = 10 * a + 5 * half + i
                own[at:at + 1, :] = answer[i][a:a + 1, 128 * half:128 * half + 128]
    packed[...] = jnp.broadcast_to(own[...][None], packed.shape)


def solve(parts):
    return pl.pallas_call(
        solve_kernel,
        name="solve",
        compiler_params=ROOM,
        out_shape=(shape((5, STAR_DEV)), shape((16, 24, 128))),
        in_specs=[VM],
        out_specs=(VM, VM),
        scratch_shapes=[pltpu.VMEM((40, 256), F32), pltpu.VMEM((24, 128), F32)],
    )(parts)


def fit_kernel(
    bounds, core, star, inv, ps, near, far, res0, res1, res2, res3, out0, out1, out2, out3, table, fit
):
    for g in range(16):
        for a in range(2):
            for half in range(2):
                rows = slice(10 * a + 5 * half, 10 * a + 5 * half + 5)
                table[4 * g + 2 * core[0] + a, :5, 128 * half:128 * half + 128] = near[g, rows, :]
                table[4 * g + 2 - 2 * core[0] + a, :5, 128 * half:128 * half + 128] = far[g, rows, :]

    def look_up(c, h_from, h0):
        ids = star[c]
        at = ids & 127
        rel = jnp.where(ids >= h_from * 256, (ids >> 7) - 2 * h0, -1)
        found = [jnp.zeros((8, 128), F32)] * 5
        for k in range(2 * HW):
            hit = rel == k
            for q in range(5):
                row = table[h0 + k // 2, q:q + 1, (k % 2) * 128:(k % 2) * 128 + 128]
                value = jnp.take_along_axis(
                    jnp.broadcast_to(row, (8, 128)), at, axis=1, mode="promise_in_bounds"
                )
                found[q] = jnp.where(hit, value, found[q])
        total = ps[c] * found[0]
        for q in range(1, 5):
            total = total + ps[q * 32 + c] * found[q]
        return total

    def chunks(n, carry):
        for u in range(PAIR):
            c = n * PAIR + u
            fit[c] = look_up(c, bounds[c], bounds[c])
        return carry

    lax.fori_loop(0, 32 // PAIR, chunks, 0)

    def rest(c, carry):
        def more(w, carry):
            h_from = bounds[c] + w * HW
            fit[c] += look_up(c, h_from, jnp.minimum(h_from, NHI - HW))
            return carry

        lax.fori_loop(1, (bounds[32 + c] - bounds[c]) // HW + 1, more, 0)
        return carry

    lax.fori_loop(0, bounds[64], rest, 0)
    total = stacked(res0, res1, res2, res3) - pick_rows(from_chunks([fit[c] for c in range(32)]).T, inv[...])
    for d, ref in enumerate((out0, out1, out2, out3)):
        ref[...] = total[d * CAP:(d + 1) * CAP]


def apply_fit(bounds, core, star, inv, ps, near, far, res):
    return pl.pallas_call(
        fit_kernel,
        name="fit",
        compiler_params=ROOM,
        out_shape=(shape((CAP, ROWS)),) * 4,
        in_specs=[SM, SM] + [VM] * 9,
        out_specs=(VM,) * 4,
        scratch_shapes=[pltpu.VMEM((NHI, 8, 256), F32), pltpu.VMEM((32, 8, 128), F32)],
    )(bounds, core, star, inv, ps, near, far, *res)


def to_sky(slabs, sign):
    n = lax.axis_size("sky")
    moved = {
        d: lax.ppermute(slabs[d], "sky", [(i, (i + sign * d) % n) for i in range(n)]) for d in (2, 1, 3)
    }
    return [slabs[0]] + [moved[d] for d in (1, 2, 3)]


def in_hbm(x):
    return pltpu.with_memory_space_constraint(x, pltpu.HBM)


def steps(attitude, win_start, design, obs_value, star_design, star_local, block_dest, block_count):
    attitude, win_start, obs_value, star_local, block_dest = map(
        in_hbm, (attitude, win_start, obs_value, star_local, block_dest)
    )
    partials = in_hbm(star_design.transpose(1, 0, 2))
    design_t = in_hbm(design.transpose(0, 2, 1))
    tm = lax.axis_size("tm")
    place = lax.axis_index("tm").astype(I32)
    core = place & 1
    swap = [(i, i ^ 1) for i in range(tm)]
    chips = [list(range(0, tm, 2)), list(range(1, tm, 2))]

    sky = lax.axis_index("sky").astype(I32)[None]
    outgoing, slots = pack(sky, block_dest, block_count, partials, star_local)
    incoming = to_sky(outgoing, 1)

    knots = lax.all_to_all(pieces(attitude, tm), "tm", 0, 0, tiled=True)
    out_res = residuals(win_start, slots, block_count, knots, obs_value, design_t)
    in_res = to_sky(out_res, 1)

    star, skt, rank, came, ps, bounds = sort_slots(incoming)
    mine, theirs = scatter(bounds, core[None], star, skt, rank, ps, in_res)
    pair_sum = mine + lax.ppermute(theirs, "tm", swap)
    parts = lax.all_to_all(pair_sum, "tm", 0, 0, tiled=True, axis_index_groups=chips)
    own_update, packed = solve(parts)
    near = lax.all_to_all(packed, "tm", 0, 0, tiled=True, axis_index_groups=chips)
    inv = invert(came)
    far = lax.ppermute(near, "tm", swap)
    updated = apply_fit(bounds, core[None], star, inv, ps, near, far, in_res)
    returned = to_sky(updated, -1)
    result = collect(slots, block_count, returned)
    return (result, own_update)


def solution(mesh):
    placed = (
        P(None, "tm"),
        P(("sky", "tm")),
        P(("sky", "tm"), None, None),
        P(("sky", "tm"), None),
        P(("sky", "tm"), None, None),
        P(("sky", "tm"), None),
        P(("sky", "tm")),
        P(("sky", "tm")),
    )
    return jax.shard_map(
        steps,
        mesh=mesh,
        in_specs=placed,
        out_specs=(P(("sky", "tm"), None), P(None, ("sky", "tm"))),
        check_vma=False,
    )
```
